32 devices in a mesh: mult: 4 (over x, core), chan: 8 (over z, y).
Axes of the slice: x: 2, y: 2, z: 4, core: 2. Of those that a mesh axis runs over, the one named last changes fastest.
Arguments:
- columns: float32 [64, 1024, 128], P('chan'), may hold values from -6 to 6
- panels: float32 [8, 2, 1024, 1024], P('mult', None, 'chan'), may hold values from -0.1875 to 0.1875
- coefficients: float32 [64, 16, 8], P('chan', None, 'mult'), may hold values from -2 to 2
- channel_cols: int32 [64, 16], P('chan'), may hold values from 0 to 63, as said below
- used_slots: int32 [64], P('chan'), may hold values from 1 to 16, as said below
- lambda_low: int32 [64, 16], P('chan'), may hold values from 0 to 3
- lambda_high: int32 [64, 16], P('chan'), may hold values from 5 to 8
- energies: float32 [64], P('chan'), may hold values from 0 to 2
- contour: float32 [2], replicated, may hold values from 0.5 to 1.5
Outputs:
- filtered: float32 [64, 1024, 128], P('chan', 'mult')
The draws below stay inside these ranges and needn't reach their ends.
Inputs may be any that keep to these rules, and one draw needn't show every extreme that they name: channel_cols[i, s] // 8 differs from i // 8 by at most 2, and channel_cols[i, 0] = i. `used_slots`: some channel uses all 16 slots.
All inputs are finite; a program needn't handle non-finite values.
Results may differ from the reference program's by a relative error of at most 0.0001.
Values sent between devices are 32-bit elements; how exact they have to be, the bound alone decides.
No kernel may reach another device: no remote copies, remote signals or barrier semaphores. Data moves between devices by JAX's collectives and lax.ppermute only.
A program may use at most 192 MiB of HBM per device.

```python
import jax
import jax.numpy as jnp
from jax import lax

NB = 1024
K = 64
NL = 8
MAXNZ = 16
R = 2
CH_DEV = 8
NCH = 64


def draw_channel_cols(key, part):
    key_offset, key_inner = jax.random.split(key)
    row_ids = jnp.arange(NCH, dtype=jnp.int32)
    own_block = row_ids // CH_DEV
    offset = jax.random.randint(key_offset, (NCH, MAXNZ), -R, R + 1)
    in_block = jax.random.randint(key_inner, (NCH, MAXNZ), 0, CH_DEV)
    target = own_block[:, None] + offset
    inside = (target >= 0) & (target < NCH // CH_DEV)
    target = jnp.where(inside, target, own_block[:, None])
    picked = target * CH_DEV + in_block
    first_slot = jnp.arange(MAXNZ, dtype=jnp.int32)[None, :] == 0
    return jnp.where(first_slot, row_ids[:, None], picked).astype(jnp.int32)


def draw_used_slots(key, part):
    key_count, key_full = jax.random.split(key)
    counts = jax.random.randint(key_count, (NCH,), 1, MAXNZ + 1)
    fullest = jax.random.randint(key_full, (), 0, NCH)
    return jnp.where(jnp.arange(NCH, dtype=jnp.int32) == fullest, MAXNZ, counts).astype(jnp.int32)


def touch_ends(entries, rng, low, largest):
    shape = entries.shape
    index_at = [jax.random.randint(jax.random.fold_in(rng, axis), (), 0, shape[axis]) for axis in range(len(shape))]
    entries = entries.at[tuple(index_at)].set(low)
    longest = shape.index(max(shape))
    index_at[longest] = (index_at[longest] + 1) % shape[longest]
    return entries.at[tuple(index_at)].set(largest)


def level_of(own_key, extent, cuts, smallest, largest):
    gain, own = 1.0, jax.random.fold_in(own_key, 6)
    for dim, parts in cuts:
        heights = jnp.exp(jax.random.uniform(jax.random.fold_in(own, dim), (parts,), jnp.float32, smallest / len(cuts), largest / len(cuts)))
        gain = gain * jnp.repeat(heights, extent[dim] // parts).reshape([-1 if axis == dim else 1 for axis in range(len(extent))])
    return gain


def scatter_about(stream_key, extent, width, reach, cuts=(), kind=jnp.bfloat16):
    result = jax.random.normal(stream_key, extent, jnp.float32) * width
    if len(cuts) > 0:
        result = level_of(stream_key, extent, cuts, -0.22, 0.18) * result
    return jnp.clip(result, min=-reach, max=reach).astype(kind)


def setup_inputs(seed: int = 0) -> dict:
    seeds = jax.random.split(jax.random.key(seed), 10)
    columns = scatter_about(seeds[0], (NCH, NB, 2 * K), 1.0, 6.0, ((0, 8),), jnp.float32)
    panels = scatter_about(seeds[1], (NL, 2, NB, NB), NB ** -0.5, 0.1875, ((0, 4), (2, 8)), jnp.float32)
    coefficients = scatter_about(seeds[2], (NCH, MAXNZ, NL), 0.15, 2.0, ((0, 8), (2, 4)), jnp.float32)
    channel_cols = draw_channel_cols(jax.random.fold_in(seeds[9], 71), 0)
    used_slots = draw_used_slots(jax.random.fold_in(seeds[9], 71), 0)
    lambda_low = touch_ends(jax.random.randint(seeds[5], (NCH, MAXNZ), 0, NL // 2), jax.random.fold_in(seeds[5], 1), 0, (NL // 2) - 1).astype(jnp.int32)
    lambda_high = touch_ends(jax.random.randint(seeds[6], (NCH, MAXNZ), NL // 2 + 1, NL + 1), jax.random.fold_in(seeds[6], 1), NL // 2 + 1, NL).astype(jnp.int32)
    energies = jnp.clip(2.0 * jax.random.uniform(seeds[7], (NCH,), jnp.float32) ** level_of(seeds[7], (NCH,), ((0, 8),), -0.2, 0.2), 0.0, 2.0)
    contour = jnp.clip(jax.random.uniform(seeds[8], (2,), jnp.float32, 0.5, 1.5), 0.5, 1.5)
    return {"columns": columns, "panels": panels, "coefficients": coefficients, "channel_cols": channel_cols, "used_slots": used_slots, "lambda_low": lambda_low, "lambda_high": lambda_high, "energies": energies, "contour": contour}


def reference(columns, panels, coefficients, channel_cols, used_slots, lambda_low, lambda_high, energies, contour):
    half_width = columns.shape[2] // 2
    slot_ids = jnp.arange(MAXNZ, dtype=jnp.int32)
    live_slot = slot_ids[None, :] < used_slots[:, None]
    lambda_ids = jnp.arange(NL, dtype=jnp.int32)
    in_range = (lambda_ids[None, None, :] >= lambda_low[:, :, None]) & (lambda_ids[None, None, :] < lambda_high[:, :, None])
    weights = jnp.where(live_slot[:, :, None] & in_range, coefficients, jnp.zeros_like(coefficients))
    one_hot = (channel_cols[:, :, None] == jnp.arange(NCH, dtype=jnp.int32)[None, None, :]).astype(columns.dtype)
    mixing = jnp.einsum('isj,isl->ijl', one_hot, weights, precision=lax.Precision.HIGHEST)

    def per_order(total, order_id):
        panel = panels[order_id]
        real_prod = jnp.einsum('ab,cbk->cak', panel[0], columns, precision=lax.Precision.HIGHEST)
        imag_prod = jnp.einsum('ab,cbk->cak', panel[1], columns, precision=lax.Precision.HIGHEST)
        product = jnp.concatenate([real_prod[..., :half_width] - imag_prod[..., half_width:], real_prod[..., half_width:] + imag_prod[..., :half_width]], axis=-1)
        mix_now = mixing[:, :, order_id]
        return total + jnp.einsum('ij,jak->iak', mix_now, product, precision=lax.Precision.HIGHEST), None

    coupled, _ = lax.scan(per_order, jnp.zeros_like(columns), jnp.arange(NL, dtype=jnp.int32))
    energy_shift = (contour[0] - energies)[:, None, None]
    imag_shift = contour[1]
    real_part = columns[..., :half_width]
    imag_part = columns[..., half_width:]
    out_real = energy_shift * real_part - imag_shift * imag_part - coupled[..., :half_width]
    out_imag = energy_shift * imag_part + imag_shift * real_part - coupled[..., half_width:]
    return jnp.concatenate([out_real, out_imag], axis=-1)
```

```python
import functools

import jax
import jax.numpy as jnp
from jax import lax
from jax.experimental import pallas as pl
from jax.experimental.pallas import tpu as pltpu
from jax.sharding import PartitionSpec as P


R = 2
SPAN = 2 * R + 1
LANES = 128
F32 = jnp.float32
BF16 = jnp.bfloat16


def ring_order(peers):
    return list(range(0, peers, 2)) + list(range(peers - 1 - peers % 2, 0, -2))


def ring_shift(value, axis, by):
    order = ring_order(lax.axis_size(axis))
    n = len(order)
    return lax.ppermute(value, axis, [(order[i], order[(i + by) % n]) for i in range(n)])


def flip(value, axis, bit):
    return lax.ppermute(value, axis, [(i, i ^ bit) for i in range(lax.axis_size(axis))])


def split(v):
    hi = v.astype(BF16)
    return hi, (v - hi.astype(F32)).astype(BF16)


def lane_group(shape, width):
    return lax.broadcasted_iota(jnp.int32, shape, len(shape) - 1) // width


def pack_kernel(sc_ref, col_ref, out_ref, *, kw):
    m = sc_ref[0]
    n_ch, rows, lanes = col_ref.shape
    groups = lanes // kw
    half = groups // 2
    grp = lane_group((rows, lanes), kw)
    re = im = None
    for j in range(n_ch):
        v = col_ref[j]
        if j:
            v = pltpu.roll(v, j * kw, 1)
        if re is None:
            re = im = v
        else:
            re = jnp.where(grp == lax.rem(m + j, groups), v, re)
            im = jnp.where(grp == lax.rem(m + half + j, groups), v, im)
    out_ref[:, :lanes] = pltpu.roll(re, lax.rem((groups - m) * kw, lanes), 1)
    out_ref[:, lanes:] = pltpu.roll(im, lax.rem((groups + half - m) * kw, lanes), 1)


def pack(columns, meta, kw):
    n_ch, nb, lanes = columns.shape
    steps = 4
    return pl.pallas_call(
        functools.partial(pack_kernel, kw=kw),
        out_shape=jax.ShapeDtypeStruct((nb, 2 * lanes), F32),
        grid_spec=pltpu.PrefetchScalarGridSpec(
            num_scalar_prefetch=1,
            grid=(steps,),
            in_specs=[pl.BlockSpec((n_ch, nb // steps, lanes), lambda g, sc: (0, g, 0))],
            out_specs=pl.BlockSpec((nb // steps, 2 * lanes), lambda g, sc: (g, 0)),
        ),
        name="pack",
    )(meta, columns)


def unit_kernel(sc_ref, *refs, n_p, kw, steps, places, fresh):
    n_x = len(places)
    p_refs, x_refs = refs[: 2 * n_p], refs[2 * n_p : 2 * (n_p + n_x)]
    a_refs = refs[2 * (n_p + n_x) : 3 * n_p + 2 * n_x]
    c_in, c_out, y_ref, w_ref, sem = refs[3 * n_p + 2 * n_x :]
    step = pl.program_id(0)
    n_l, _, rows, _ = p_refs[0].shape
    n_chan, n_ch, _ = a_refs[0].shape
    fetch = None if fresh else pltpu.make_async_copy(c_in, w_ref, sem.at[0])

    @pl.when(step == 0)
    def _():
        if fresh:
            w_ref[...] = jnp.zeros_like(w_ref)
        else:
            fetch.start()

    parts = []
    for part in range(2):
        v = jnp.concatenate(
            [
                jnp.concatenate([p_refs[2 * a + t][l, part] for t in range(2)], axis=1)
                for a in range(n_p)
                for l in range(n_l)
            ],
            axis=0,
        )
        h, l = split(v)
        parts += [h, h, l]
    lhs = jnp.concatenate(parts, axis=1)
    rhs = []
    for t in range(n_x):
        x = jnp.concatenate([x_refs[2 * t][...], x_refs[2 * t + 1][...]], axis=0)
        lanes = x.shape[1] // 2
        xh, xl = split(x)
        yh = jnp.concatenate([-xh[:, lanes:], xh[:, :lanes]], axis=1)
        yl = jnp.concatenate([-xl[:, lanes:], xl[:, :lanes]], axis=1)
        rhs.append(jnp.concatenate([xh, xl, xh, yh, yl, yh], axis=0))
    prod = jnp.dot(lhs, jnp.concatenate(rhs, axis=1), preferred_element_type=F32)
    for t in range(n_x):
        piece = prod[:, 2 * lanes * t : 2 * lanes * (t + 1)]

        @pl.when(step == 0)
        def _():
            y_ref[t] = piece

        @pl.when(step > 0)
        def _():
            y_ref[t] += piece

    @pl.when(step == steps - 1)
    def _():
        n = n_p * n_l
        wide = SPAN * lanes
        spread = (
            lane_group((LANES, wide), kw) == lax.broadcasted_iota(jnp.int32, (LANES, wide), 0)
        ).astype(BF16)
        same = (
            lax.broadcasted_iota(jnp.int32, (1, kw, wide), 2) % kw
            == lax.broadcasted_iota(jnp.int32, (1, kw, wide), 1)
        )
        grp = lane_group((n_ch, LANES), n_ch)

        def kron(c):
            t = jnp.dot(c, spread, preferred_element_type=F32)
            t = jnp.where(same, t[:, None, :], 0.0)
            return t.reshape(n * n_ch * kw, wide).astype(BF16)

        if not fresh:
            fetch.wait()

        @pl.loop(0, n_x)
        def _(t):
            s = sc_ref[places[0] + t]
            coef = []
            for a_ref in a_refs:
                v = None
                for d in range(SPAN):
                    at = s + d - R
                    own = a_ref[jnp.clip(at, 0, n_chan - 1)]
                    own = jnp.where((at >= 0) & (at < n_chan), own, 0.0)
                    v = own if v is None else jnp.where(lax.rem(grp, LANES // n_l // n_ch) == d, own, v)
                coef += [pltpu.roll(v, LANES - l * (LANES // n_l), 1) if l else v for l in range(n_l)]
            ch, cl = split(jnp.concatenate(coef, axis=0))
            kh, kl = kron(ch), kron(cl)
            y = y_ref[t]
            z = jnp.concatenate(
                [
                    jnp.concatenate(
                        [y[i * rows : (i + 1) * rows, part * lanes : (part + 1) * lanes] for i in range(n)],
                        axis=1,
                    )
                    for part in range(2)
                ],
                axis=0,
            )
            zh, zl = split(z)
            out = jnp.dot(
                jnp.concatenate([zh, zh, zl], axis=1),
                jnp.concatenate([kh, kl, kh], axis=0),
                preferred_element_type=F32,
            )
            for d in range(SPAN):
                w_ref[s + d] += out[:, d * lanes : (d + 1) * lanes]

        back = pltpu.make_async_copy(w_ref, c_out, sem.at[1])
        back.start()
        back.wait()


def unit(total, shape, panel_sets, coefs, chunks, meta, kw):
    n_l, _, rows, nb = panel_sets[0].shape
    half = nb // 2
    steps = max(1, half // LANES)
    blk = half // steps
    wide = chunks[0][0].shape[1]
    n = len(panel_sets)
    in_specs, args = [], []
    for p in panel_sets:
        in_specs += [
            pl.BlockSpec((n_l, 2, rows, blk), lambda g, sc: (0, 0, 0, g)),
            pl.BlockSpec((n_l, 2, rows, blk), lambda g, sc: (0, 0, 0, steps + g)),
        ]
        args += [p, p]
    for top, bottom, _ in chunks:
        off = steps if bottom.shape[0] == nb else 0
        in_specs += [
            pl.BlockSpec((blk, wide), lambda g, sc: (g, 0)),
            pl.BlockSpec((blk, wide), lambda g, sc, off=off: (off + g, 0)),
        ]
        args += [top, bottom]
    fresh = total is None
    if fresh:
        total = coefs[0]
    in_specs += [pl.BlockSpec(c.shape, lambda g, sc: (0, 0, 0)) for c in coefs]
    in_specs += [pl.BlockSpec(memory_space=pltpu.HBM)]
    args += [*coefs, total]
    flops = 2 * 3 * n * n_l * rows * wide * (2 * nb + SPAN * LANES) * len(chunks)
    return pl.pallas_call(
        functools.partial(
            unit_kernel, n_p=n, kw=kw, steps=steps, places=tuple(c[2] for c in chunks), fresh=fresh
        ),
        out_shape=jax.ShapeDtypeStruct(shape, F32),
        grid_spec=pltpu.PrefetchScalarGridSpec(
            num_scalar_prefetch=1,
            grid=(steps,),
            in_specs=in_specs,
            out_specs=pl.BlockSpec(memory_space=pltpu.HBM),
            scratch_shapes=[
                pltpu.VMEM((len(chunks), n * n_l * rows, wide), F32),
                pltpu.VMEM(shape, F32),
                pltpu.SemaphoreType.DMA((2,)),
            ],
        ),
        input_output_aliases={} if fresh else {len(args): 0},
        cost_estimate=pl.CostEstimate(
            flops=flops, transcendentals=0, bytes_accessed=4 * n * n_l * 2 * rows * nb
        ),
        compiler_params=pltpu.CompilerParams(vmem_limit_bytes=48 << 20),
        name="unit",
    )(meta, *[pltpu.with_memory_space_constraint(a, pltpu.HBM) for a in args])


def finish_kernel(sc_ref, energy_ref, contour_ref, col_ref, *refs, kw, n_mult):
    pieces, out_ref, held = refs[:-2], refs[-2], refs[-1]
    n_ch, _, lanes = col_ref.shape
    n = len(pieces)
    per = n // n_mult
    me = sc_ref[1]
    for s in range(n):
        held[lax.rem(me - s + n, n)] = pieces[s][...]
    rows = pieces[0].shape[0] // 2
    groups = 2 * n_mult
    grp = lane_group((rows, lanes), kw)
    upper = lax.broadcasted_iota(jnp.int32, (rows, lanes), 1) >= lanes // 2
    shift = contour_ref[1]
    for h in range(per):
        vs = [held[u * per + h, part * rows : (part + 1) * rows] for part in range(2) for u in range(n_mult)]
        dist = 1
        while dist < groups:
            odd = (grp // dist) % 2 == 1
            nxt = list(vs)
            for a in range(groups):
                if not a & dist:
                    b = a + dist
                    nxt[a] = jnp.where(odd, pltpu.roll(vs[b], dist * kw, 1), vs[a])
                    nxt[b] = jnp.where(odd, vs[b], pltpu.roll(vs[a], lanes - dist * kw, 1))
            vs = nxt
            dist *= 2
        at = pl.ds(h * rows, rows)
        for i in range(n_ch):
            x = col_ref[i, at]
            turned = pltpu.roll(x, lanes // 2, 1)
            turned = jnp.where(upper, turned, -turned)
            out_ref[i, at] = (contour_ref[0] - energy_ref[i]) * x + shift * turned - vs[i]


def finish(pieces, columns, energies, contour, meta, kw, n_mult):
    n_ch, nb, lanes = columns.shape
    out_rows = nb // n_mult
    smem = pl.BlockSpec(memory_space=pltpu.SMEM)
    return pl.pallas_call(
        functools.partial(finish_kernel, kw=kw, n_mult=n_mult),
        out_shape=jax.ShapeDtypeStruct((n_ch, out_rows, lanes), F32),
        grid_spec=pltpu.PrefetchScalarGridSpec(
            num_scalar_prefetch=1,
            grid=(1,),
            in_specs=[smem, smem, pl.BlockSpec((n_ch, out_rows, lanes), lambda g, sc: (0, sc[0], 0))]
            + [pl.BlockSpec(p.shape, lambda g, sc: (0, 0)) for p in pieces],
            out_specs=pl.BlockSpec((n_ch, out_rows, lanes), lambda g, sc: (0, 0, 0)),
            scratch_shapes=[pltpu.VMEM((len(pieces),) + pieces[0].shape, F32)],
        ),
        name="finish",
    )(meta, energies, contour, columns, *pieces)


def mixing_blocks(coefficients, channel_cols, used_slots, lambda_low, lambda_high, chan_index, mult_index):
    n_ch, slots, lam = coefficients.shape
    n_chan = lax.axis_size("chan")
    local = channel_cols - (chan_index - R) * n_ch
    slot_ids = jnp.arange(slots, dtype=jnp.int32)
    live = slot_ids[None, :] < used_slots[:, None]
    lambda_ids = mult_index * lam + jnp.arange(lam, dtype=jnp.int32)
    inside = (lambda_ids >= lambda_low[:, :, None]) & (lambda_ids < lambda_high[:, :, None])
    weights = jnp.where(live[:, :, None] & inside, coefficients, jnp.zeros_like(coefficients))
    lane = jnp.arange(LANES, dtype=jnp.int32)
    stride = LANES // lam
    order, dist = lane // stride, (lane % stride) // n_ch
    want = (SPAN - 1 - dist)[None, :] * n_ch + jnp.arange(n_ch, dtype=jnp.int32)[:, None]
    want = jnp.where(dist[None, :] < SPAN, want, -1)
    by_lane = jnp.tile(local.T, (1, LANES // n_ch))
    w_lane = jnp.zeros((slots, LANES), F32)
    for l in range(lam):
        w_lane = jnp.where(order[None, :] == l, jnp.tile(weights[:, :, l].T, (1, LANES // n_ch)), w_lane)
    mine = jnp.sum(
        jnp.where(by_lane[:, None, :] == want[None], w_lane[:, None, :], 0.0), axis=0
    )
    return jnp.broadcast_to(mine[None], (n_chan,) + mine.shape)


def steps_of(n_chan):
    full = (n_chan - 1) // 2
    return full, max(1, min(2, full - 1))


def body(
    columns,
    panels,
    coefficients,
    channel_cols,
    used_slots,
    lambda_low,
    lambda_high,
    energies,
    contour,
):
    _, nb, lanes = columns.shape
    n_chan, n_mult = lax.axis_size("chan"), lax.axis_size("mult")
    chan_index, mult_index = lax.axis_index("chan"), lax.axis_index("mult")
    kw = lanes // 2 // n_mult
    rows = panels.shape[2]

    seq = ring_order(n_chan)
    hops = [0]
    for step in range(1, n_chan // 2 + 1):
        hops += [-step, step]
    table = jnp.asarray(
        [[i] + [seq[(seq.index(i) + by) % n_chan] for by in hops] for i in range(n_chan)], jnp.int32
    )
    meta = jnp.concatenate([mult_index[None], table[chan_index]])

    def spot(by):
        return 2 + hops.index(by)

    sent = mixing_blocks(
        coefficients, channel_cols, used_slots, lambda_low, lambda_high, chan_index, mult_index
    )
    sent, meta = lax.optimization_barrier((sent, meta))
    near_coefs = [lax.all_to_all(sent, "chan", 0, 0, tiled=True)]
    near_coefs[0], meta = lax.optimization_barrier((near_coefs[0], meta))
    mine = pack(columns, meta, kw)

    near_sets = [panels]
    bit = n_mult // 4
    while bit:
        near_sets += [flip(p, "mult", bit) for p in near_sets]
        near_coefs += [flip(p, "mult", bit) for p in near_coefs]
        bit //= 2
    far = [flip(panels, "mult", n_mult // 2)]
    far_coefs = [flip(c, "mult", n_mult // 2) for c in near_coefs]

    shape = (n_chan + 2 * R, 2 * rows, LANES)

    def add(total, sets, coefs, chunks):
        return unit(total, shape, sets, coefs, chunks, meta, kw)

    full_steps, switch = steps_of(n_chan)
    total = None
    ahead = behind = mine
    held = [(mine, mine, spot(0))]
    total = add(total, near_sets, near_coefs, held)
    for step in range(1, full_steps + 1):
        ahead = ring_shift(ahead, "chan", 1)
        behind = ring_shift(behind, "chan", -1)
        new = [(ahead, ahead, spot(-step)), (behind, behind, spot(step))]
        if step <= switch:
            total = add(total, near_sets, near_coefs, new)
            held += new
        else:
            total = add(total, near_sets + far, near_coefs + far_coefs, new)
        if step == switch:
            far[0], total = lax.optimization_barrier((far[0], total))
            bit = n_mult // 4
            while bit:
                far += [flip(p, "mult", bit) for p in far]
                bit //= 2
            for at in range(0, len(held), 3):
                total = add(total, far, far_coefs, held[at : at + 3])
    if n_chan % 2 == 0:
        top = ring_shift(ahead[: nb // 2], "chan", 1)
        bottom = ring_shift(behind[nb // 2 :], "chan", -1)
        total = add(total, near_sets + far, near_coefs + far_coefs, [(top, bottom, spot(n_chan // 2))])

    per = n_chan // n_mult
    mine_q = mult_index * per + lax.rem(chan_index, per)
    pieces = []
    for s in range(n_chan):
        pairs = []
        for m in range(n_mult):
            for c in range(n_chan):
                q = m * per + c % per
                pairs.append((m * n_chan + c, (c // per) * n_chan + (q + s) % n_chan))
        piece = lax.dynamic_index_in_dim(total, R + lax.rem(mine_q + s, n_chan), 0, keepdims=False)
        pieces.append(lax.ppermute(piece, ("mult", "chan"), pairs))
    return finish(pieces, columns, energies, contour, meta, kw, n_mult)


def solution(mesh):
    return jax.shard_map(
        body,
        mesh=mesh,
        in_specs=(
            P("chan", None, None),
            P("mult", None, "chan", None),
            P("chan", None, "mult"),
            P("chan", None),
            P("chan"),
            P("chan", None),
            P("chan", None),
            P("chan"),
            P(),
        ),
        out_specs=P("chan", "mult", None),
        check_vma=False,
    )
```

```python
import functools

import jax
import jax.numpy as jnp
from jax import lax
from jax.experimental import pallas as pl
from jax.experimental.pallas import tpu as pltpu
from jax.sharding import PartitionSpec as P


R = 2
SPAN = 2 * R + 1
LANES = 128
F32 = jnp.float32
BF16 = jnp.bfloat16


def ring_order(peers):
    return list(range(0, peers, 2)) + list(range(peers - 1 - peers % 2, 0, -2))


def ring_shift(value, axis, by):
    order = ring_order(lax.axis_size(axis))
    n = len(order)
    return lax.ppermute(value, axis, [(order[i], order[(i + by) % n]) for i in range(n)])


def flip(value, axis, bit):
    return lax.ppermute(value, axis, [(i, i ^ bit) for i in range(lax.axis_size(axis))])


def split(v):
    hi = v.astype(BF16)
    return hi, (v - hi.astype(F32)).astype(BF16)


def lane_group(shape, width):
    return lax.broadcasted_iota(jnp.int32, shape, len(shape) - 1) // width


def pack_kernel(sc_ref, col_ref, out_ref, *, kw):
    n_ch, rows, lanes = col_ref.shape
    groups = lanes // kw
    half = groups // 2
    sub = min(rows, 64)
    grp = lane_group((sub, lanes), kw)

    def share(m):
        @pl.loop(0, rows // sub)
        def _(t):
            at = pl.ds(pl.multiple_of(t * sub, sub), sub)
            re = im = None
            for j in range(n_ch):
                v = col_ref[j, at]
                if j:
                    v = pltpu.roll(v, j * kw, 1)
                re = v if re is None else jnp.where(grp == (m + j) % groups, v, re)
                im = v if im is None else jnp.where(grp == (m + half + j) % groups, v, im)
            out_ref[at, :lanes] = pltpu.roll(re, (groups - m) * kw, 1) if m else re
            out_ref[at, lanes:] = pltpu.roll(im, (half - m) * kw, 1)

    for m in range(half):
        pl.when(sc_ref[0] == m)(functools.partial(share, m))


def pack(columns, meta, kw, part):
    n_ch, nb, lanes = columns.shape
    nb, steps = nb // 2, 2
    return pl.pallas_call(
        functools.partial(pack_kernel, kw=kw),
        out_shape=jax.ShapeDtypeStruct((nb, 2 * lanes), F32),
        grid_spec=pltpu.PrefetchScalarGridSpec(
            num_scalar_prefetch=1,
            grid=(steps,),
            in_specs=[pl.BlockSpec((n_ch, nb // steps, lanes), lambda g, sc: (0, part * steps + g, 0))],
            out_specs=pl.BlockSpec((nb // steps, 2 * lanes), lambda g, sc: (g, 0)),
        ),
        name="pack",
    )(meta, columns)


def unit_kernel(sc_ref, *refs, n_p, kw, steps, places, fresh):
    n_x = len(places)
    p_refs, x_refs = refs[: 2 * n_p], refs[2 * n_p : 2 * (n_p + n_x)]
    a_refs = refs[2 * (n_p + n_x) : 3 * n_p + 2 * n_x]
    c_in, c_out, y_ref, w_ref, sem = refs[3 * n_p + 2 * n_x :]
    step = pl.program_id(0)
    n_l, _, rows, _ = p_refs[0].shape
    n_chan, n_ch, _ = a_refs[0].shape
    if fresh:
        fetch = None
    elif n_x == 1:
        near = pl.ds(sc_ref[places[0]], SPAN)
        fetch = pltpu.make_async_copy(c_in.at[near], w_ref, sem.at[0])
    else:
        fetch = pltpu.make_async_copy(c_in, w_ref, sem.at[0])

    @pl.when(step == 0)
    def _():
        if fresh:
            w_ref[...] = jnp.zeros_like(w_ref)
        else:
            fetch.start()

    parts = []
    for part in range(2):
        v = jnp.concatenate(
            [
                jnp.concatenate([p_refs[2 * a + t][l, part] for t in range(2)], axis=1)
                for a in range(n_p)
                for l in range(n_l)
            ],
            axis=0,
        )
        h, l = split(v)
        parts.append((h, l))
    (rh, rl), (ih, il) = parts
    rhs = []
    for t in range(n_x):
        x = jnp.concatenate([x_refs[2 * t][...], x_refs[2 * t + 1][...]], axis=0)
        lanes = x.shape[1] // 2
        xh, xl = split(x)
        yh = jnp.concatenate([-xh[:, lanes:], xh[:, :lanes]], axis=1)
        yl = jnp.concatenate([-xl[:, lanes:], xl[:, :lanes]], axis=1)
        rhs.append((jnp.concatenate([xh, yh], axis=0), jnp.concatenate([xl, yl], axis=0)))
    hi = jnp.concatenate([rh, ih], axis=1)
    lo = jnp.concatenate([rl, il], axis=1)
    if n_x == 1:
        both = jnp.dot(hi, jnp.concatenate(rhs[0], axis=1), preferred_element_type=F32)
        prod = both[:, : 2 * lanes] + both[:, 2 * lanes :]
        prod += jnp.dot(lo, rhs[0][0], preferred_element_type=F32)
    else:
        prod = jnp.dot(
            jnp.concatenate([hi, hi, lo], axis=1),
            jnp.concatenate([jnp.concatenate([h, l, h], axis=0) for h, l in rhs], axis=1),
            preferred_element_type=F32,
        )
    for t in range(n_x):
        piece = prod[:, 2 * lanes * t : 2 * lanes * (t + 1)]

        @pl.when(step == 0)
        def _():
            y_ref[t] = piece

        @pl.when(step > 0)
        def _():
            y_ref[t] += piece

    @pl.when(step == steps - 1)
    def _():
        n = n_p * n_l
        wide = SPAN * lanes
        spread = (
            lane_group((LANES, wide), kw) == lax.broadcasted_iota(jnp.int32, (LANES, wide), 0)
        ).astype(BF16)
        same = (
            lax.broadcasted_iota(jnp.int32, (1, kw, wide), 2) % kw
            == lax.broadcasted_iota(jnp.int32, (1, kw, wide), 1)
        )
        grp = lane_group((n_ch, LANES), n_ch)

        def kron(c):
            t = jnp.dot(c, spread, preferred_element_type=F32)
            t = jnp.where(same, t[:, None, :], 0.0)
            return t.reshape(n * n_ch * kw, wide).astype(BF16)

        if not fresh:
            fetch.wait()

        @pl.loop(0, n_x)
        def _(t):
            s = sc_ref[places[0] + t]
            me = sc_ref[1]
            coef = []
            for a_ref in a_refs:
                v = None
                for d in range(SPAN):
                    at = s + d - R
                    own = a_ref[lax.rem(me - at + 2 * n_chan, n_chan)]
                    own = jnp.where((at >= 0) & (at < n_chan), own, 0.0)
                    v = own if v is None else jnp.where(lax.rem(grp, LANES // n_l // n_ch) == d, own, v)
                coef += [pltpu.roll(v, LANES - l * (LANES // n_l), 1) if l else v for l in range(n_l)]
            ch, cl = split(jnp.concatenate(coef, axis=0))
            kh, kl = kron(ch), kron(cl)
            y = y_ref[t]
            z = jnp.concatenate(
                [
                    jnp.concatenate(
                        [y[i * rows : (i + 1) * rows, part * lanes : (part + 1) * lanes] for i in range(n)],
                        axis=1,
                    )
                    for part in range(2)
                ],
                axis=0,
            )
            zh, zl = split(z)
            out = jnp.dot(
                jnp.concatenate([zh, zh, zl], axis=1),
                jnp.concatenate([kh, kl, kh], axis=0),
                preferred_element_type=F32,
            )
            for d in range(SPAN):
                w_ref[d if n_x == 1 and not fresh else s + d] += out[:, d * lanes : (d + 1) * lanes]

        if n_x == 1 and not fresh:
            back = pltpu.make_async_copy(w_ref, c_out.at[near], sem.at[1])
        else:
            back = pltpu.make_async_copy(w_ref, c_out, sem.at[1])
        back.start()
        back.wait()


def unit(total, shape, panel_sets, coefs, chunks, meta, kw):
    n_l, _, rows, nb = panel_sets[0].shape
    half = nb // 2
    steps = max(1, half // LANES)
    blk = half // steps
    wide = chunks[0][0].shape[1]
    n = len(panel_sets)
    in_specs, args = [], []
    for p in panel_sets:
        in_specs += [
            pl.BlockSpec((n_l, 2, rows, blk), lambda g, sc: (0, 0, 0, g)),
            pl.BlockSpec((n_l, 2, rows, blk), lambda g, sc: (0, 0, 0, steps + g)),
        ]
        args += [p, p]
    for top, bottom, _ in chunks:
        off = steps if bottom.shape[0] == nb else 0
        in_specs += [
            pl.BlockSpec((blk, wide), lambda g, sc: (g, 0)),
            pl.BlockSpec((blk, wide), lambda g, sc, off=off: (off + g, 0)),
        ]
        args += [top, bottom]
    fresh = total is None
    if fresh:
        total = coefs[0]
    in_specs += [pl.BlockSpec(c.shape, lambda g, sc: (0, 0, 0)) for c in coefs]
    in_specs += [pl.BlockSpec(memory_space=pltpu.HBM)]
    args += [*coefs, total]
    flops = 2 * 3 * n * n_l * rows * wide * (2 * nb + SPAN * LANES) * len(chunks)
    return pl.pallas_call(
        functools.partial(
            unit_kernel, n_p=n, kw=kw, steps=steps, places=tuple(c[2] for c in chunks), fresh=fresh
        ),
        out_shape=jax.ShapeDtypeStruct(shape, F32),
        grid_spec=pltpu.PrefetchScalarGridSpec(
            num_scalar_prefetch=1,
            grid=(steps,),
            in_specs=in_specs,
            out_specs=pl.BlockSpec(memory_space=pltpu.HBM),
            scratch_shapes=[
                pltpu.VMEM((len(chunks), n * n_l * rows, wide), F32),
                pltpu.VMEM((SPAN,) + shape[1:] if len(chunks) == 1 and not fresh else shape, F32),
                pltpu.SemaphoreType.DMA((2,)),
            ],
        ),
        input_output_aliases={} if fresh else {len(args): 0},
        cost_estimate=pl.CostEstimate(
            flops=flops, transcendentals=0, bytes_accessed=4 * n * n_l * 2 * rows * nb
        ),
        compiler_params=pltpu.CompilerParams(vmem_limit_bytes=26 << 20),
        name="unit",
    )(
        meta,
        *args[: 2 * n],
        *[pltpu.with_memory_space_constraint(a, pltpu.HBM) for a in args[2 * n :]],
    )


def shift_kernel(sc_ref, energy_ref, contour_ref, col_ref, out_ref):
    n_ch, rows, lanes = col_ref.shape
    upper = lax.broadcasted_iota(jnp.int32, (rows, lanes), 1) >= lanes // 2
    shift = jnp.where(upper, contour_ref[1], -contour_ref[1])
    for i in range(n_ch):
        x = col_ref[i]
        out_ref[i] = (contour_ref[0] - energy_ref[i]) * x + shift * pltpu.roll(x, lanes // 2, 1)


def shifted_columns(columns, energies, contour, meta, n_mult):
    n_ch, nb, lanes = columns.shape
    rows = nb // n_mult
    steps = max(1, rows // 64)
    sub = rows // steps
    smem = pl.BlockSpec(memory_space=pltpu.SMEM)
    return pl.pallas_call(
        shift_kernel,
        out_shape=jax.ShapeDtypeStruct((n_ch, rows, lanes), F32),
        grid_spec=pltpu.PrefetchScalarGridSpec(
            num_scalar_prefetch=1,
            grid=(steps,),
            in_specs=[smem, smem, pl.BlockSpec((n_ch, sub, lanes), lambda g, sc: (0, sc[0] * steps + g, 0))],
            out_specs=pl.BlockSpec((n_ch, sub, lanes), lambda g, sc: (0, g, 0)),
        ),
        name="shifted",
    )(meta, energies, contour, columns)


def finish_kernel(sc_ref, base_ref, *refs, kw, n_mult):
    pieces, out_ref, held = refs[:-2], refs[-2], refs[-1]
    n_ch, per, sub, lanes = base_ref.shape
    n = len(pieces)
    me = sc_ref[1]
    for s in range(n):
        held[lax.rem(me - s + n, n)] = pieces[s][...]
    groups = 2 * n_mult
    v = jnp.concatenate(
        [
            jnp.concatenate([held[u * per + h, part] for part in range(2) for u in range(n_mult)], axis=1)
            for h in range(per)
        ],
        axis=0,
    )
    vh, vl = split(v)
    both = jnp.concatenate([vh, vl], axis=0)
    row = lax.broadcasted_iota(jnp.int32, (groups * lanes, lanes), 0)
    col = lax.broadcasted_iota(jnp.int32, (groups * lanes, lanes), 1)
    start = (col // kw) * lanes + col % kw
    picks = jnp.concatenate([(row == start + i * kw).astype(BF16) for i in range(n_ch)], axis=1)
    out = jnp.dot(both, picks, preferred_element_type=F32)
    out = out[: per * sub] + out[per * sub :]
    for h in range(per):
        for i in range(n_ch):
            out_ref[i, h] = base_ref[i, h] - out[h * sub : (h + 1) * sub, i * lanes : (i + 1) * lanes]


def finish(pieces, base, meta, kw, n_mult):
    n_ch, out_rows, lanes = base.shape
    rows = pieces[0].shape[0] // 2
    per = out_rows // rows
    sub = min(rows, 64)
    out = pl.pallas_call(
        functools.partial(finish_kernel, kw=kw, n_mult=n_mult),
        out_shape=jax.ShapeDtypeStruct((n_ch, per, rows, lanes), F32),
        grid_spec=pltpu.PrefetchScalarGridSpec(
            num_scalar_prefetch=1,
            grid=(rows // sub,),
            in_specs=[pl.BlockSpec((n_ch, per, sub, lanes), lambda g, sc: (0, 0, g, 0))]
            + [pl.BlockSpec((2, sub, lanes), lambda g, sc: (0, g, 0)) for _ in pieces],
            out_specs=pl.BlockSpec((n_ch, per, sub, lanes), lambda g, sc: (0, 0, g, 0)),
            scratch_shapes=[pltpu.VMEM((len(pieces), 2, sub, lanes), F32)],
        ),
        name="finish",
    )(meta, base.reshape(n_ch, per, rows, lanes), *[p.reshape(2, rows, lanes) for p in pieces])
    return out.reshape(n_ch, out_rows, lanes)


def mixing_blocks(coefficients, channel_cols, used_slots, lambda_low, lambda_high, chan_index, mult_index):
    n_ch, slots, lam = coefficients.shape
    local = channel_cols - (chan_index - R) * n_ch
    slot_ids = jnp.arange(slots, dtype=jnp.int32)
    live = slot_ids[None, :] < used_slots[:, None]
    lambda_ids = mult_index * lam + jnp.arange(lam, dtype=jnp.int32)
    inside = (lambda_ids >= lambda_low[:, :, None]) & (lambda_ids < lambda_high[:, :, None])
    weights = jnp.where(live[:, :, None] & inside, coefficients, jnp.zeros_like(coefficients))
    lane = jnp.arange(LANES, dtype=jnp.int32)
    stride = LANES // lam
    order, dist = lane // stride, (lane % stride) // n_ch
    want = (SPAN - 1 - dist)[None, :] * n_ch + jnp.arange(n_ch, dtype=jnp.int32)[:, None]
    want = jnp.where(dist[None, :] < SPAN, want, -1)
    by_lane = jnp.tile(local.T, (1, LANES // n_ch))
    w_lane = jnp.zeros((slots, LANES), F32)
    for l in range(lam):
        w_lane = jnp.where(order[None, :] == l, jnp.tile(weights[:, :, l].T, (1, LANES // n_ch)), w_lane)
    mine = jnp.sum(
        jnp.where(by_lane[:, None, :] == want[None], w_lane[:, None, :], 0.0), axis=0
    )
    return mine


def steps_of(n_chan):
    full = (n_chan - 1) // 2
    return full, min(2, full)


def body(
    columns,
    panels,
    coefficients,
    channel_cols,
    used_slots,
    lambda_low,
    lambda_high,
    energies,
    contour,
):
    _, _, lanes = columns.shape
    n_chan, n_mult = lax.axis_size("chan"), lax.axis_size("mult")
    chan_index, mult_index = lax.axis_index("chan"), lax.axis_index("mult")
    kw = lanes // 2 // n_mult
    rows = panels.shape[2]

    seq = ring_order(n_chan)
    hops = [0]
    for step in range(1, n_chan // 2 + 1):
        hops += [-step, step]
    table = jnp.asarray(
        [[i] + [seq[(seq.index(i) + by) % n_chan] for by in hops] for i in range(n_chan)], jnp.int32
    )
    meta = jnp.concatenate([mult_index[None], table[chan_index]])

    def spot(by):
        return 2 + hops.index(by)

    mine = []
    for part in range(2):
        mine.append(pack(columns, meta, kw, part))
    mine[1], coefficients = lax.optimization_barrier((mine[1], coefficients))
    sent = mixing_blocks(
        coefficients, channel_cols, used_slots, lambda_low, lambda_high, chan_index, mult_index
    )
    near_coefs = [sent]
    for by in range(1, n_chan):
        near_coefs.append(
            lax.ppermute(sent, "chan", [(i, (i + by) % n_chan) for i in range(n_chan)])
        )
    near_coefs = [jnp.stack(near_coefs)]

    near_sets = [panels]
    bit = n_mult // 4
    while bit:
        near_sets += [flip(p, "mult", bit) for p in near_sets]
        near_coefs += [flip(p, "mult", bit) for p in near_coefs]
        bit //= 2
    far = [flip(panels, "mult", n_mult // 2)]
    far_coefs = [flip(c, "mult", n_mult // 2) for c in near_coefs]

    shape = (n_chan + 2 * R, 2 * rows, LANES)

    def add(total, sets, coefs, chunks):
        return unit(total, shape, sets, coefs, chunks, meta, kw)

    full_steps, switch = steps_of(n_chan)
    total = None
    ahead, behind = list(mine), list(mine)
    held, late = [(*mine, spot(0))], []
    for step in range(1, full_steps + 1):
        for part in range(2):
            ahead[part] = ring_shift(ahead[part], "chan", 1)
            behind[part] = ring_shift(behind[part], "chan", -1)
        held += [(*ahead, spot(-step)), (*behind, spot(step))]
        if step <= switch:
            total = add(total, near_sets, near_coefs, held)
            late += held
        else:
            total = add(total, near_sets + far, near_coefs + far_coefs, held)
        held = []
        if step == 1:
            far[0], total = lax.optimization_barrier((far[0], total))
            bit = n_mult // 4
            while bit:
                far += [flip(p, "mult", bit) for p in far]
                bit //= 2
        if step == switch:
            total = add(total, far, far_coefs, late)
    if n_chan % 2 == 0:
        top = ring_shift(ahead[0], "chan", 1)
        bottom = ring_shift(behind[1], "chan", -1)
        total = add(total, near_sets + far, near_coefs + far_coefs, [(top, bottom, spot(n_chan // 2))])

    per = n_chan // n_mult
    mine_q = mult_index * per + lax.rem(chan_index, per)
    pieces = []
    for s in range(n_chan):
        pairs = []
        for m in range(n_mult):
            for c in range(n_chan):
                q = m * per + c % per
                pairs.append((m * n_chan + c, (c // per) * n_chan + (q + s) % n_chan))
        piece = lax.dynamic_index_in_dim(total, R + lax.rem(mine_q + s, n_chan), 0, keepdims=False)
        pieces.append(lax.ppermute(piece, ("mult", "chan"), pairs))
    base = shifted_columns(columns, energies, contour, meta, n_mult)
    return finish(pieces, base, meta, kw, n_mult)


def solution(mesh):
    return jax.shard_map(
        body,
        mesh=mesh,
        in_specs=(
            P("chan", None, None),
            P("mult", None, "chan", None),
            P("chan", None, "mult"),
            P("chan", None),
            P("chan"),
            P("chan", None),
            P("chan", None),
            P("chan"),
            P(),
        ),
        out_specs=P("chan", "mult", None),
        check_vma=False,
    )
```

```python
import functools

import jax
import jax.numpy as jnp
from jax import lax
from jax.experimental import pallas as pl
from jax.experimental.pallas import tpu as pltpu
from jax.sharding import PartitionSpec as P


R = 2
SPAN = 2 * R + 1
LANES = 128
F32 = jnp.float32
BF16 = jnp.bfloat16


def ring_order(peers):
    return list(range(0, peers, 2)) + list(range(peers - 1 - peers % 2, 0, -2))


def ring_shift(value, axis, by):
    order = ring_order(lax.axis_size(axis))
    n = len(order)
    return lax.ppermute(value, axis, [(order[i], order[(i + by) % n]) for i in range(n)])


def flip(value, axis, bit):
    return lax.ppermute(value, axis, [(i, i ^ bit) for i in range(lax.axis_size(axis))])


def split(v):
    hi = v.astype(BF16)
    return hi, (v - hi.astype(F32)).astype(BF16)


def lane_group(shape, width):
    return lax.broadcasted_iota(jnp.int32, shape, len(shape) - 1) // width


def pack_kernel(col_ref, out_ref, *, kw):
    n_ch, rows, lanes = col_ref.shape
    groups = lanes // kw
    half = groups // 2
    sub = min(rows, 64)
    grp = lane_group((sub, lanes), kw)

    def share(m):
        @pl.loop(0, rows // sub)
        def _(t):
            at = pl.ds(pl.multiple_of(t * sub, sub), sub)
            re = im = None
            for j in range(n_ch):
                v = col_ref[j, at]
                if j:
                    v = pltpu.roll(v, j * kw, 1)
                re = v if re is None else jnp.where(grp == (m + j) % groups, v, re)
                im = v if im is None else jnp.where(grp == (m + half + j) % groups, v, im)
            out_ref[at, :lanes] = pltpu.roll(re, (groups - m) * kw, 1) if m else re
            out_ref[at, lanes:] = pltpu.roll(im, (half - m) * kw, 1)

    for m in range(half):
        pl.when(lax.axis_index("mult") == m)(functools.partial(share, m))


def pack(columns, kw, part):
    n_ch, nb, lanes = columns.shape
    nb, steps = nb // 2, 2
    return pl.pallas_call(
        functools.partial(pack_kernel, kw=kw),
        out_shape=jax.ShapeDtypeStruct((nb, 2 * lanes), F32),
        grid=(steps,),
        in_specs=[pl.BlockSpec((n_ch, nb // steps, lanes), lambda g: (0, part * steps + g, 0))],
        out_specs=pl.BlockSpec((nb // steps, 2 * lanes), lambda g: (g, 0)),
        name="pack",
    )(columns)


def unit_kernel(sc_ref, *refs, n_p, kw, steps, places, fresh, emit):
    n_x = len(places)
    p_refs, x_refs = refs[: 2 * n_p], refs[2 * n_p : 2 * (n_p + n_x)]
    a_refs = refs[2 * (n_p + n_x) : 3 * n_p + 2 * n_x]
    c_in, *c_outs, y_ref, w_ref, sem = refs[3 * n_p + 2 * n_x :]
    step = pl.program_id(0)
    n_l, _, rows, _ = p_refs[0].shape
    n_chan, n_ch, _ = a_refs[0].shape
    if fresh:
        fetch = None
    else:
        fetch = pltpu.make_async_copy(c_in, w_ref, sem.at[0])

    @pl.when(step == 0)
    def _():
        if fresh:
            w_ref[...] = jnp.zeros_like(w_ref)
        else:
            fetch.start()

    parts = []
    for part in range(2):
        v = jnp.concatenate(
            [
                jnp.concatenate([p_refs[2 * a + t][l, part] for t in range(2)], axis=1)
                for a in range(n_p)
                for l in range(n_l)
            ],
            axis=0,
        )
        h, l = split(v)
        parts.append((h, l))
    (rh, rl), (ih, il) = parts
    rhs = []
    for t in range(n_x):
        x = jnp.concatenate([x_refs[2 * t][...], x_refs[2 * t + 1][...]], axis=0)
        lanes = x.shape[1] // 2
        xh, xl = split(x)
        yh = jnp.concatenate([-xh[:, lanes:], xh[:, :lanes]], axis=1)
        yl = jnp.concatenate([-xl[:, lanes:], xl[:, :lanes]], axis=1)
        rhs.append((jnp.concatenate([xh, yh], axis=0), jnp.concatenate([xl, yl], axis=0)))
    hi = jnp.concatenate([rh, ih], axis=1)
    lo = jnp.concatenate([rl, il], axis=1)
    if n_x == 1:
        both = jnp.dot(hi, jnp.concatenate(rhs[0], axis=1), preferred_element_type=F32)
        prod = both[:, : 2 * lanes] + both[:, 2 * lanes :]
        prod += jnp.dot(lo, rhs[0][0], preferred_element_type=F32)
    else:
        prod = jnp.dot(
            jnp.concatenate([hi, hi, lo], axis=1),
            jnp.concatenate([jnp.concatenate([h, l, h], axis=0) for h, l in rhs], axis=1),
            preferred_element_type=F32,
        )
    for t in range(n_x):
        piece = prod[:, 2 * lanes * t : 2 * lanes * (t + 1)]

        @pl.when(step == 0)
        def _():
            y_ref[t] = piece

        @pl.when(step > 0)
        def _():
            y_ref[t] += piece

    @pl.when(step == steps - 1)
    def _():
        n = n_p * n_l
        wide = SPAN * lanes
        spread = (
            lane_group((LANES, wide), kw) == lax.broadcasted_iota(jnp.int32, (LANES, wide), 0)
        ).astype(BF16)
        same = (
            lax.broadcasted_iota(jnp.int32, (1, kw, wide), 2) % kw
            == lax.broadcasted_iota(jnp.int32, (1, kw, wide), 1)
        )
        grp = lane_group((n_ch, LANES), n_ch)

        def kron(c):
            t = jnp.dot(c, spread, preferred_element_type=F32)
            t = jnp.broadcast_to(t.astype(BF16)[:, None, :], (n * n_ch, kw, wide))
            return jnp.where(same, t, jnp.zeros_like(t)).reshape(n * n_ch * kw, wide)

        if not fresh:
            fetch.wait()

        @pl.loop(0, n_x)
        def _(t):
            s = sc_ref[places[0] + t]
            me = sc_ref[1]
            coef = []
            for a_ref in a_refs:
                v = None
                for d in range(SPAN):
                    at = s + d - R
                    own = a_ref[lax.rem(me - at + 2 * n_chan, n_chan)]
                    own = jnp.where((at >= 0) & (at < n_chan), own, 0.0)
                    v = own if v is None else jnp.where(lax.rem(grp, LANES // n_l // n_ch) == d, own, v)
                coef += [pltpu.roll(v, LANES - l * (LANES // n_l), 1) if l else v for l in range(n_l)]
            ch, cl = split(jnp.concatenate(coef, axis=0))
            kh, kl = kron(ch), kron(cl)
            y = y_ref[t]
            z = jnp.concatenate(
                [
                    jnp.concatenate(
                        [y[i * rows : (i + 1) * rows, part * lanes : (part + 1) * lanes] for i in range(n)],
                        axis=1,
                    )
                    for part in range(2)
                ],
                axis=0,
            )
            zh, zl = split(z)
            out = jnp.dot(
                jnp.concatenate([zh, zh, zl], axis=1),
                jnp.concatenate([kh, kl, kh], axis=0),
                preferred_element_type=F32,
            )
            for d in range(SPAN):
                w_ref[s + d] += out[:, d * lanes : (d + 1) * lanes]

        backs = []
        for t, c_out in enumerate(c_outs):
            block = w_ref
            if emit:
                per = n_chan // emit
                block = w_ref.at[R + lax.rem(sc_ref[0] * per + lax.rem(sc_ref[1], per) + t, n_chan)]
            backs.append(pltpu.make_async_copy(block, c_out, sem.at[1 + t]))
            backs[-1].start()
        for back in backs:
            back.wait()


def unit(total, shape, panel_sets, coefs, chunks, meta, kw, emit=0):
    n_l, _, rows, nb = panel_sets[0].shape
    half = nb // 2
    steps = max(1, half // (2 * LANES))
    blk = half // steps
    wide = chunks[0][0].shape[1]
    n = len(panel_sets)
    in_specs, args = [], []
    for p in panel_sets:
        in_specs += [
            pl.BlockSpec((n_l, 2, rows, blk), lambda g, sc: (0, 0, 0, g)),
            pl.BlockSpec((n_l, 2, rows, blk), lambda g, sc: (0, 0, 0, steps + g)),
        ]
        args += [p, p]
    for top, bottom, _ in chunks:
        off = steps if bottom.shape[0] == nb else 0
        in_specs += [
            pl.BlockSpec((blk, wide), lambda g, sc: (g, 0)),
            pl.BlockSpec((blk, wide), lambda g, sc, off=off: (off + g, 0)),
        ]
        args += [top, bottom]
    fresh = total is None
    if fresh:
        total = coefs[0]
    in_specs += [pl.BlockSpec(c.shape, lambda g, sc: (0, 0, 0)) for c in coefs]
    in_specs += [pl.BlockSpec(memory_space=pltpu.HBM)]
    args += [*coefs, total]
    flops = 2 * 3 * n * n_l * rows * wide * (2 * nb + SPAN * LANES) * len(chunks)
    n_chan = shape[0] - 2 * R
    outs = [jax.ShapeDtypeStruct(shape[1:], F32)] * n_chan if emit else [jax.ShapeDtypeStruct(shape, F32)]
    result = pl.pallas_call(
        functools.partial(
            unit_kernel, n_p=n, kw=kw, steps=steps, places=tuple(c[2] for c in chunks), fresh=fresh, emit=emit
        ),
        out_shape=outs,
        grid_spec=pltpu.PrefetchScalarGridSpec(
            num_scalar_prefetch=1,
            grid=(steps,),
            in_specs=in_specs,
            out_specs=[pl.BlockSpec(memory_space=pltpu.HBM) for _ in outs],
            scratch_shapes=[
                pltpu.VMEM((len(chunks), n * n_l * rows, wide), F32),
                pltpu.VMEM(shape, F32),
                pltpu.SemaphoreType.DMA((1 + len(outs),)),
            ],
        ),
        input_output_aliases={} if fresh or emit else {len(args): 0},
        cost_estimate=pl.CostEstimate(
            flops=flops, transcendentals=0, bytes_accessed=4 * n * n_l * 2 * rows * nb
        ),
        compiler_params=pltpu.CompilerParams(vmem_limit_bytes=40 << 20),
        name="unit",
    )(
        meta,
        *args[: 2 * n],
        *[pltpu.with_memory_space_constraint(a, pltpu.HBM) for a in args[2 * n :]],
    )
    return result if emit else result[0]


def shift_kernel(sc_ref, energy_ref, contour_ref, col_ref, out_ref):
    n_ch, rows, lanes = col_ref.shape
    upper = lax.broadcasted_iota(jnp.int32, (rows, lanes), 1) >= lanes // 2
    shift = jnp.where(upper, contour_ref[1], -contour_ref[1])
    for i in range(n_ch):
        x = col_ref[i]
        out_ref[i] = (contour_ref[0] - energy_ref[i]) * x + shift * pltpu.roll(x, lanes // 2, 1)


def shifted_columns(columns, energies, contour, meta, n_mult):
    n_ch, nb, lanes = columns.shape
    rows = nb // n_mult
    steps = max(1, rows // 64)
    sub = rows // steps
    smem = pl.BlockSpec(memory_space=pltpu.SMEM)
    return pl.pallas_call(
        shift_kernel,
        out_shape=jax.ShapeDtypeStruct((n_ch, rows, lanes), F32),
        grid_spec=pltpu.PrefetchScalarGridSpec(
            num_scalar_prefetch=1,
            grid=(steps,),
            in_specs=[smem, smem, pl.BlockSpec((n_ch, sub, lanes), lambda g, sc: (0, sc[0] * steps + g, 0))],
            out_specs=pl.BlockSpec((n_ch, sub, lanes), lambda g, sc: (0, g, 0)),
        ),
        name="shifted",
    )(meta, energies, contour, columns)


def finish_kernel(sc_ref, base_ref, *refs, kw, n_mult):
    pieces, (out_ref, held, pick_ref) = refs[:-3], refs[-3:]
    n_ch, per, sub, lanes = base_ref.shape
    n = len(pieces)
    me = sc_ref[1]
    for s in range(n):
        held[lax.rem(me - s + n, n)] = pieces[s][...]
    groups = 2 * n_mult
    v = jnp.concatenate(
        [
            jnp.concatenate([held[u * per + h, part] for part in range(2) for u in range(n_mult)], axis=1)
            for h in range(per)
        ],
        axis=0,
    )
    vh, vl = split(v)
    both = jnp.concatenate([vh, vl], axis=0)

    @pl.when(pl.program_id(0) == 0)
    def _():
        row = lax.broadcasted_iota(jnp.int32, (groups * lanes, lanes), 0)
        col = lax.broadcasted_iota(jnp.int32, (groups * lanes, lanes), 1)
        start = (col // kw) * lanes + col % kw
        for i in range(n_ch):
            pick_ref[:, i * lanes : (i + 1) * lanes] = (row == start + i * kw).astype(BF16)

    out = jnp.dot(both, pick_ref[...], preferred_element_type=F32)
    out = out[: per * sub] + out[per * sub :]
    for h in range(per):
        for i in range(n_ch):
            out_ref[i, h] = base_ref[i, h] - out[h * sub : (h + 1) * sub, i * lanes : (i + 1) * lanes]


def finish(pieces, base, meta, kw, n_mult):
    n_ch, out_rows, lanes = base.shape
    rows = pieces[0].shape[0] // 2
    per = out_rows // rows
    sub = min(rows, 64)
    out = pl.pallas_call(
        functools.partial(finish_kernel, kw=kw, n_mult=n_mult),
        out_shape=jax.ShapeDtypeStruct((n_ch, per, rows, lanes), F32),
        grid_spec=pltpu.PrefetchScalarGridSpec(
            num_scalar_prefetch=1,
            grid=(rows // sub,),
            in_specs=[pl.BlockSpec((n_ch, per, sub, lanes), lambda g, sc: (0, 0, g, 0))]
            + [pl.BlockSpec((2, sub, lanes), lambda g, sc: (0, g, 0)) for _ in pieces],
            out_specs=pl.BlockSpec((n_ch, per, sub, lanes), lambda g, sc: (0, 0, g, 0)),
            scratch_shapes=[
                pltpu.VMEM((len(pieces), 2, sub, lanes), F32),
                pltpu.VMEM((2 * n_mult * lanes, n_ch * lanes), BF16),
            ],
        ),
        name="finish",
    )(
        meta,
        base.reshape(n_ch, per, rows, lanes),
        *[pltpu.with_memory_space_constraint(p.reshape(2, rows, lanes), pltpu.HBM) for p in pieces],
    )
    return out.reshape(n_ch, out_rows, lanes)


def mixing_blocks(coefficients, channel_cols, used_slots, lambda_low, lambda_high, chan_index, mult_index):
    n_ch, slots, lam = coefficients.shape
    local = channel_cols - (chan_index - R) * n_ch
    slot_ids = jnp.arange(slots, dtype=jnp.int32)
    live = slot_ids[None, :] < used_slots[:, None]
    lambda_ids = mult_index * lam + jnp.arange(lam, dtype=jnp.int32)
    inside = (lambda_ids >= lambda_low[:, :, None]) & (lambda_ids < lambda_high[:, :, None])
    weights = jnp.where(live[:, :, None] & inside, coefficients, jnp.zeros_like(coefficients))
    lane = jnp.arange(LANES, dtype=jnp.int32)
    stride = LANES // lam
    order, dist = lane // stride, (lane % stride) // n_ch
    want = (SPAN - 1 - dist)[None, :] * n_ch + jnp.arange(n_ch, dtype=jnp.int32)[:, None]
    want = jnp.where(dist[None, :] < SPAN, want, -1)
    by_lane = jnp.tile(local.T, (1, LANES // n_ch))
    w_lane = jnp.zeros((slots, LANES), F32)
    for l in range(lam):
        w_lane = jnp.where(order[None, :] == l, jnp.tile(weights[:, :, l].T, (1, LANES // n_ch)), w_lane)
    mine = jnp.sum(
        jnp.where(by_lane[:, None, :] == want[None], w_lane[:, None, :], 0.0), axis=0
    )
    return mine


def steps_of(n_chan):
    full = (n_chan - 1) // 2
    return full, min(2, full)


def body(
    columns,
    panels,
    coefficients,
    channel_cols,
    used_slots,
    lambda_low,
    lambda_high,
    energies,
    contour,
):
    _, _, lanes = columns.shape
    n_chan, n_mult = lax.axis_size("chan"), lax.axis_size("mult")
    chan_index, mult_index = lax.axis_index("chan"), lax.axis_index("mult")
    kw = lanes // 2 // n_mult
    rows = panels.shape[2]

    seq = ring_order(n_chan)
    hops = [0]
    for step in range(1, n_chan // 2 + 1):
        hops += [-step, step]
    table = jnp.asarray(
        [[i] + [seq[(seq.index(i) + by) % n_chan] for by in hops] for i in range(n_chan)], jnp.int32
    )
    meta = jnp.concatenate([mult_index[None], table[chan_index]])

    def spot(by):
        return 2 + hops.index(by)

    mine = []
    for part in range(2):
        mine.append(pack(columns, kw, part))
    mine[1], coefficients = lax.optimization_barrier((mine[1], coefficients))
    sent = mixing_blocks(
        coefficients, channel_cols, used_slots, lambda_low, lambda_high, chan_index, mult_index
    )
    near_coefs = [sent]
    for by in range(1, n_chan):
        near_coefs.append(
            lax.ppermute(sent, "chan", [(i, (i + by) % n_chan) for i in range(n_chan)])
        )
    near_coefs = [jnp.stack(near_coefs)]

    near_sets = [panels]
    bit = n_mult // 4
    while bit:
        near_sets += [flip(p, "mult", bit) for p in near_sets]
        near_coefs += [flip(p, "mult", bit) for p in near_coefs]
        bit //= 2
    far = [flip(panels, "mult", n_mult // 2)]
    far_coefs = [flip(c, "mult", n_mult // 2) for c in near_coefs]

    shape = (n_chan + 2 * R, 2 * rows, LANES)

    def add(total, sets, coefs, chunks, emit=0):
        return unit(total, shape, sets, coefs, chunks, meta, kw, emit)

    full_steps, switch = steps_of(n_chan)
    total = None
    ahead, behind = list(mine), list(mine)
    held, late = [(*mine, spot(0))], []
    for step in range(1, full_steps + 1):
        for part in range(2):
            ahead[part] = ring_shift(ahead[part], "chan", 1)
            behind[part] = ring_shift(behind[part], "chan", -1)
        held += [(*ahead, spot(-step)), (*behind, spot(step))]
        if step <= switch:
            total = add(total, near_sets, near_coefs, held)
            late += held
        else:
            total = add(total, near_sets + far, near_coefs + far_coefs, held)
        held = []
        if step == 1:
            far[0], total = lax.optimization_barrier((far[0], total))
            bit = n_mult // 4
            while bit:
                far += [flip(p, "mult", bit) for p in far]
                bit //= 2
        if step == switch:
            total = add(total, far, far_coefs, late)
    top = ring_shift(ahead[0], "chan", 1)
    bottom = ring_shift(behind[1], "chan", -1)
    sends = add(
        total, near_sets + far, near_coefs + far_coefs, [(top, bottom, spot(n_chan // 2))], n_mult
    )

    per = n_chan // n_mult
    pieces = []
    for s in range(n_chan):
        pairs = []
        for m in range(n_mult):
            for c in range(n_chan):
                q = m * per + c % per
                pairs.append((m * n_chan + c, (c // per) * n_chan + (q + s) % n_chan))
        pieces.append(lax.ppermute(sends[s], ("mult", "chan"), pairs))
    base = shifted_columns(columns, energies, contour, meta, n_mult)
    return finish(pieces, base, meta, kw, n_mult)


def solution(mesh):
    return jax.shard_map(
        body,
        mesh=mesh,
        in_specs=(
            P("chan", None, None),
            P("mult", None, "chan", None),
            P("chan", None, "mult"),
            P("chan", None),
            P("chan"),
            P("chan", None),
            P("chan", None),
            P("chan"),
            P(),
        ),
        out_specs=P("chan", "mult", None),
        check_vma=False,
    )
```

```python
import functools

import jax
import jax.numpy as jnp
from jax import lax
from jax.experimental import pallas as pl
from jax.experimental.pallas import tpu as pltpu
from jax.sharding import PartitionSpec as P


R = 2
SPAN = 2 * R + 1
LANES = 128
F32 = jnp.float32
BF16 = jnp.bfloat16


def ring_order(peers):
    return list(range(0, peers, 2)) + list(range(peers - 1 - peers % 2, 0, -2))


def ring_shift(value, axis, by):
    order = ring_order(lax.axis_size(axis))
    n = len(order)
    return lax.ppermute(value, axis, [(order[i], order[(i + by) % n]) for i in range(n)])


def flip(value, axis, bit):
    return lax.ppermute(value, axis, [(i, i ^ bit) for i in range(lax.axis_size(axis))])


def split(v):
    hi = v.astype(BF16)
    return hi, (v - hi.astype(F32)).astype(BF16)


def lane_group(shape, width):
    return lax.broadcasted_iota(jnp.int32, shape, len(shape) - 1) // width


def pack_kernel(col_ref, out_ref, *, kw):
    n_ch, rows, lanes = col_ref.shape
    groups = lanes // kw
    half = groups // 2
    sub = min(rows, 64)
    grp = lane_group((sub, lanes), kw)

    def share(m):
        @pl.loop(0, rows // sub)
        def _(t):
            at = pl.ds(pl.multiple_of(t * sub, sub), sub)
            re = im = None
            for j in range(n_ch):
                v = col_ref[j, at]
                if j:
                    v = pltpu.roll(v, j * kw, 1)
                re = v if re is None else jnp.where(grp == (m + j) % groups, v, re)
                im = v if im is None else jnp.where(grp == (m + half + j) % groups, v, im)
            out_ref[at, :lanes] = pltpu.roll(re, (groups - m) * kw, 1) if m else re
            out_ref[at, lanes:] = pltpu.roll(im, (half - m) * kw, 1)

    for m in range(half):
        pl.when(lax.axis_index("mult") == m)(functools.partial(share, m))


def pack(columns, kw, part):
    n_ch, nb, lanes = columns.shape
    nb, steps = nb // 2, 2
    return pl.pallas_call(
        functools.partial(pack_kernel, kw=kw),
        out_shape=jax.ShapeDtypeStruct((nb, 2 * lanes), F32),
        grid=(steps,),
        in_specs=[pl.BlockSpec((n_ch, nb // steps, lanes), lambda g: (0, part * steps + g, 0))],
        out_specs=pl.BlockSpec((nb // steps, 2 * lanes), lambda g: (g, 0)),
        name="pack",
    )(columns)


def unit_kernel(sc_ref, *refs, n_p, kw, steps, places, fresh, emit):
    n_x = len(places)
    p_refs, x_refs = refs[: 2 * n_p], refs[2 * n_p : 2 * (n_p + n_x)]
    a_refs = refs[2 * (n_p + n_x) : 3 * n_p + 2 * n_x]
    c_in, *c_outs, y_ref, w_ref, sem = refs[3 * n_p + 2 * n_x :]
    step = pl.program_id(0)
    n_l, _, rows, _ = p_refs[0].shape
    n_chan, n_ch, _ = a_refs[0].shape
    if fresh:
        fetch = None
    else:
        fetch = pltpu.make_async_copy(c_in, w_ref, sem.at[0])

    @pl.when(step == 0)
    def _():
        if fresh:
            w_ref[...] = jnp.zeros_like(w_ref)
        else:
            fetch.start()

    parts = []
    for part in range(2):
        v = jnp.concatenate(
            [
                jnp.concatenate([p_refs[2 * a + t][l, part] for t in range(2)], axis=1)
                for a in range(n_p)
                for l in range(n_l)
            ],
            axis=0,
        )
        h, l = split(v)
        parts.append((h, l))
    (rh, rl), (ih, il) = parts
    rhs = []
    for t in range(n_x):
        x = jnp.concatenate([x_refs[2 * t][...], x_refs[2 * t + 1][...]], axis=0)
        lanes = x.shape[1] // 2
        xh, xl = split(x)
        yh = jnp.concatenate([-xh[:, lanes:], xh[:, :lanes]], axis=1)
        yl = jnp.concatenate([-xl[:, lanes:], xl[:, :lanes]], axis=1)
        rhs.append((jnp.concatenate([xh, yh], axis=0), jnp.concatenate([xl, yl], axis=0)))
    hi = jnp.concatenate([rh, ih], axis=1)
    lo = jnp.concatenate([rl, il], axis=1)
    if n_x == 1:
        both = jnp.dot(hi, jnp.concatenate(rhs[0], axis=1), preferred_element_type=F32)
        prod = both[:, : 2 * lanes] + both[:, 2 * lanes :]
        prod += jnp.dot(lo, rhs[0][0], preferred_element_type=F32)
    else:
        prod = jnp.dot(
            jnp.concatenate([hi, hi, lo], axis=1),
            jnp.concatenate([jnp.concatenate([h, l, h], axis=0) for h, l in rhs], axis=1),
            preferred_element_type=F32,
        )
    for t in range(n_x):
        piece = prod[:, 2 * lanes * t : 2 * lanes * (t + 1)]

        @pl.when(step == 0)
        def _():
            y_ref[t] = piece

        @pl.when(step > 0)
        def _():
            y_ref[t] += piece

    @pl.when(step == steps - 1)
    def _():
        n = n_p * n_l
        wide = SPAN * lanes
        spread = (
            lane_group((LANES, wide), kw) == lax.broadcasted_iota(jnp.int32, (LANES, wide), 0)
        ).astype(BF16)
        same = (
            lax.broadcasted_iota(jnp.int32, (1, kw, wide), 2) % kw
            == lax.broadcasted_iota(jnp.int32, (1, kw, wide), 1)
        )
        grp = lane_group((n_ch, LANES), n_ch)

        def kron(c):
            t = jnp.dot(c, spread, preferred_element_type=F32)
            t = jnp.broadcast_to(t.astype(BF16)[:, None, :], (n * n_ch, kw, wide))
            return jnp.where(same, t, jnp.zeros_like(t)).reshape(n * n_ch * kw, wide)

        if not fresh:
            fetch.wait()

        @pl.loop(0, n_x)
        def _(t):
            s = sc_ref[places[0] + t]
            me = sc_ref[1]
            coef = []
            for a_ref in a_refs:
                v = None
                for d in range(SPAN):
                    at = s + d - R
                    own = a_ref[lax.rem(me - at + 2 * n_chan, n_chan)]
                    own = jnp.where((at >= 0) & (at < n_chan), own, 0.0)
                    v = own if v is None else jnp.where(lax.rem(grp, LANES // n_l // n_ch) == d, own, v)
                coef += [pltpu.roll(v, LANES - l * (LANES // n_l), 1) if l else v for l in range(n_l)]
            ch, cl = split(jnp.concatenate(coef, axis=0))
            kh, kl = kron(ch), kron(cl)
            y = y_ref[t]
            z = jnp.concatenate(
                [
                    jnp.concatenate(
                        [y[i * rows : (i + 1) * rows, part * lanes : (part + 1) * lanes] for i in range(n)],
                        axis=1,
                    )
                    for part in range(2)
                ],
                axis=0,
            )
            zh, zl = split(z)
            out = jnp.dot(
                jnp.concatenate([zh, zh, zl], axis=1),
                jnp.concatenate([kh, kl, kh], axis=0),
                preferred_element_type=F32,
            )
            for d in range(SPAN):
                w_ref[s + d] += out[:, d * lanes : (d + 1) * lanes]

        backs = []
        for t, c_out in enumerate(c_outs):
            block = w_ref
            if emit:
                per = n_chan // emit
                block = w_ref.at[R + lax.rem(sc_ref[0] * per + lax.rem(sc_ref[1], per) + t, n_chan)]
            backs.append(pltpu.make_async_copy(block, c_out, sem.at[1 + t]))
            backs[-1].start()
        for back in backs:
            back.wait()


def unit(total, shape, panel_sets, coefs, chunks, meta, kw, emit=0, kept=False):
    n_l, _, rows, nb = panel_sets[0].shape
    half = nb // 2
    steps = max(1, half // (2 * LANES))
    blk = half // steps
    wide = chunks[0][0].shape[1]
    n = len(panel_sets)
    in_specs, args = [], []
    for p in panel_sets:
        in_specs += [
            pl.BlockSpec((n_l, 2, rows, blk), lambda g, sc: (0, 0, 0, g)),
            pl.BlockSpec((n_l, 2, rows, blk), lambda g, sc: (0, 0, 0, steps + g)),
        ]
        args += [p, p]
    for top, bottom, _ in chunks:
        off = steps if bottom.shape[0] == nb else 0
        in_specs += [
            pl.BlockSpec((blk, wide), lambda g, sc: (g, 0)),
            pl.BlockSpec((blk, wide), lambda g, sc, off=off: (off + g, 0)),
        ]
        args += [top, bottom]
    fresh = total is None
    if fresh:
        total = coefs[0]
    in_specs += [pl.BlockSpec(c.shape, lambda g, sc: (0, 0, 0)) for c in coefs]
    in_specs += [pl.BlockSpec(memory_space=pl.ANY)]
    args += [*coefs, total]
    flops = 2 * 3 * n * n_l * rows * wide * (2 * nb + SPAN * LANES) * len(chunks)
    n_chan = shape[0] - 2 * R
    outs = [jax.ShapeDtypeStruct(shape[1:], F32)] * n_chan if emit else [jax.ShapeDtypeStruct(shape, F32)]
    result = pl.pallas_call(
        functools.partial(
            unit_kernel, n_p=n, kw=kw, steps=steps, places=tuple(c[2] for c in chunks), fresh=fresh, emit=emit
        ),
        out_shape=outs,
        grid_spec=pltpu.PrefetchScalarGridSpec(
            num_scalar_prefetch=1,
            grid=(steps,),
            in_specs=in_specs,
            out_specs=[pl.BlockSpec(memory_space=pl.ANY) for _ in outs],
            scratch_shapes=[
                pltpu.VMEM((len(chunks), n * n_l * rows, wide), F32),
                pltpu.VMEM(shape, F32),
                pltpu.SemaphoreType.DMA((1 + len(outs),)),
            ],
        ),
        input_output_aliases={} if fresh or emit else {len(args): 0},
        cost_estimate=pl.CostEstimate(
            flops=flops, transcendentals=0, bytes_accessed=4 * n * n_l * 2 * rows * nb
        ),
        compiler_params=pltpu.CompilerParams(vmem_limit_bytes=30 << 20),
        name="unit",
    )(
        meta,
        *args[: 2 * n],
        *[pltpu.with_memory_space_constraint(a, pltpu.HBM) if kept else a for a in args[2 * n : -n - 1]],
        *args[-n - 1 :],
    )
    return result if emit else result[0]


def shift_kernel(sc_ref, energy_ref, contour_ref, col_ref, out_ref):
    n_ch, rows, lanes = col_ref.shape
    upper = lax.broadcasted_iota(jnp.int32, (rows, lanes), 1) >= lanes // 2
    shift = jnp.where(upper, contour_ref[1], -contour_ref[1])
    for i in range(n_ch):
        x = col_ref[i]
        out_ref[i] = (contour_ref[0] - energy_ref[i]) * x + shift * pltpu.roll(x, lanes // 2, 1)


def shifted_columns(columns, energies, contour, meta, n_mult):
    n_ch, nb, lanes = columns.shape
    rows = nb // n_mult
    steps = max(1, rows // 64)
    sub = rows // steps
    smem = pl.BlockSpec(memory_space=pltpu.SMEM)
    return pl.pallas_call(
        shift_kernel,
        out_shape=jax.ShapeDtypeStruct((n_ch, rows, lanes), F32),
        grid_spec=pltpu.PrefetchScalarGridSpec(
            num_scalar_prefetch=1,
            grid=(steps,),
            in_specs=[smem, smem, pl.BlockSpec((n_ch, sub, lanes), lambda g, sc: (0, sc[0] * steps + g, 0))],
            out_specs=pl.BlockSpec((n_ch, sub, lanes), lambda g, sc: (0, g, 0)),
        ),
        name="shifted",
    )(meta, energies, contour, columns)


def finish_kernel(sc_ref, base_ref, *refs, kw, n_mult):
    pieces, out_ref, held = refs[:-2], refs[-2], refs[-1]
    n_ch, per, sub, lanes = base_ref.shape
    n = len(pieces)
    me = sc_ref[1]
    for s in range(n):
        held[lax.rem(me - s + n, n)] = pieces[s][...]
    groups = 2 * n_mult
    v = jnp.concatenate(
        [
            jnp.concatenate([held[u * per + h, part] for part in range(2) for u in range(n_mult)], axis=1)
            for h in range(per)
        ],
        axis=0,
    )
    vh, vl = split(v)
    both = jnp.concatenate([vh, vl], axis=0)

    row = lax.broadcasted_iota(jnp.int32, (groups * lanes, lanes), 0)
    col = lax.broadcasted_iota(jnp.int32, (groups * lanes, lanes), 1)
    start = (col // kw) * lanes + col % kw
    picks = jnp.concatenate([(row == start + i * kw).astype(BF16) for i in range(n_ch)], axis=1)
    out = jnp.dot(both, picks, preferred_element_type=F32)
    out = out[: per * sub] + out[per * sub :]
    for h in range(per):
        for i in range(n_ch):
            out_ref[i, h] = base_ref[i, h] - out[h * sub : (h + 1) * sub, i * lanes : (i + 1) * lanes]


def finish(pieces, base, meta, kw, n_mult):
    n_ch, out_rows, lanes = base.shape
    rows = pieces[0].shape[0] // 2
    per = out_rows // rows
    sub = min(rows, 64)
    out = pl.pallas_call(
        functools.partial(finish_kernel, kw=kw, n_mult=n_mult),
        out_shape=jax.ShapeDtypeStruct((n_ch, per, rows, lanes), F32),
        grid_spec=pltpu.PrefetchScalarGridSpec(
            num_scalar_prefetch=1,
            grid=(rows // sub,),
            in_specs=[pl.BlockSpec((n_ch, per, sub, lanes), lambda g, sc: (0, 0, g, 0))]
            + [pl.BlockSpec((2, sub, lanes), lambda g, sc: (0, g, 0)) for _ in pieces],
            out_specs=pl.BlockSpec((n_ch, per, sub, lanes), lambda g, sc: (0, 0, g, 0)),
            scratch_shapes=[pltpu.VMEM((len(pieces), 2, sub, lanes), F32)],
        ),
        name="finish",
    )(
        meta,
        base.reshape(n_ch, per, rows, lanes),
        *[p.reshape(2, rows, lanes) for p in pieces],
    )
    return out.reshape(n_ch, out_rows, lanes)


def mixing_blocks(coefficients, channel_cols, used_slots, lambda_low, lambda_high, chan_index, mult_index):
    n_ch, slots, lam = coefficients.shape
    local = channel_cols - (chan_index - R) * n_ch
    slot_ids = jnp.arange(slots, dtype=jnp.int32)
    live = slot_ids[None, :] < used_slots[:, None]
    lambda_ids = mult_index * lam + jnp.arange(lam, dtype=jnp.int32)
    inside = (lambda_ids >= lambda_low[:, :, None]) & (lambda_ids < lambda_high[:, :, None])
    weights = jnp.where(live[:, :, None] & inside, coefficients, jnp.zeros_like(coefficients))
    lane = jnp.arange(LANES, dtype=jnp.int32)
    stride = LANES // lam
    order, dist = lane // stride, (lane % stride) // n_ch
    want = (SPAN - 1 - dist)[None, :] * n_ch + jnp.arange(n_ch, dtype=jnp.int32)[:, None]
    want = jnp.where(dist[None, :] < SPAN, want, -1)
    by_lane = jnp.tile(local.T, (1, LANES // n_ch))
    w_lane = jnp.zeros((slots, LANES), F32)
    for l in range(lam):
        w_lane = jnp.where(order[None, :] == l, jnp.tile(weights[:, :, l].T, (1, LANES // n_ch)), w_lane)
    mine = jnp.sum(
        jnp.where(by_lane[:, None, :] == want[None], w_lane[:, None, :], 0.0), axis=0
    )
    return mine


def steps_of(n_chan):
    full = (n_chan - 1) // 2
    return full, min(2, full)


def body(
    columns,
    panels,
    coefficients,
    channel_cols,
    used_slots,
    lambda_low,
    lambda_high,
    energies,
    contour,
):
    _, _, lanes = columns.shape
    n_chan, n_mult = lax.axis_size("chan"), lax.axis_size("mult")
    chan_index, mult_index = lax.axis_index("chan"), lax.axis_index("mult")
    kw = lanes // 2 // n_mult
    rows = panels.shape[2]

    seq = ring_order(n_chan)
    hops = [0]
    for step in range(1, n_chan // 2 + 1):
        hops += [-step, step]
    table = jnp.asarray(
        [[i] + [seq[(seq.index(i) + by) % n_chan] for by in hops] for i in range(n_chan)], jnp.int32
    )
    meta = jnp.concatenate([mult_index[None], table[chan_index]])

    def spot(by):
        return 2 + hops.index(by)

    mine = []
    for part in range(2):
        mine.append(pack(columns, kw, part))
    mine[1], coefficients = lax.optimization_barrier((mine[1], coefficients))
    sent = mixing_blocks(
        coefficients, channel_cols, used_slots, lambda_low, lambda_high, chan_index, mult_index
    )
    near_coefs = [sent]
    for by in range(1, n_chan):
        near_coefs.append(
            lax.ppermute(sent, "chan", [(i, (i + by) % n_chan) for i in range(n_chan)])
        )
    near_coefs = [jnp.stack(near_coefs)]

    near_sets = [panels]
    bit = n_mult // 4
    while bit:
        near_sets += [flip(p, "mult", bit) for p in near_sets]
        near_coefs += [flip(p, "mult", bit) for p in near_coefs]
        bit //= 2
    far = [flip(panels, "mult", n_mult // 2)]
    far_coefs = [flip(c, "mult", n_mult // 2) for c in near_coefs]

    shape = (n_chan + 2 * R, 2 * rows, LANES)

    def add(total, sets, coefs, chunks, emit=0, kept=False):
        return unit(total, shape, sets, coefs, chunks, meta, kw, emit, kept)

    full_steps, switch = steps_of(n_chan)
    total = None
    ahead, behind = list(mine), list(mine)
    held, late = [(*mine, spot(0))], []
    for step in range(1, full_steps + 1):
        for part in range(2):
            ahead[part] = ring_shift(ahead[part], "chan", 1)
            behind[part] = ring_shift(behind[part], "chan", -1)
        held += [(*ahead, spot(-step)), (*behind, spot(step))]
        if step <= switch:
            total = add(total, near_sets, near_coefs, held)
            late += held
        else:
            total = add(total, near_sets + far, near_coefs + far_coefs, held)
        held = []
        if step == 1:
            far[0], total = lax.optimization_barrier((far[0], total))
            bit = n_mult // 4
            while bit:
                far += [flip(p, "mult", bit) for p in far]
                bit //= 2
        if step == switch:
            total = add(total, far, far_coefs, late)
    top = ring_shift(ahead[0], "chan", 1)
    bottom = ring_shift(behind[1], "chan", -1)
    sends = add(
        total, near_sets + far, near_coefs + far_coefs, [(top, bottom, spot(n_chan // 2))], n_mult
    )

    per = n_chan // n_mult
    pieces = []
    for s in range(n_chan):
        pairs = []
        for m in range(n_mult):
            for c in range(n_chan):
                q = m * per + c % per
                pairs.append((m * n_chan + c, (c // per) * n_chan + (q + s) % n_chan))
        pieces.append(lax.ppermute(sends[s], ("mult", "chan"), pairs))
    base = shifted_columns(columns, energies, contour, meta, n_mult)
    return finish(pieces, base, meta, kw, n_mult)


def solution(mesh):
    return jax.shard_map(
        body,
        mesh=mesh,
        in_specs=(
            P("chan", None, None),
            P("mult", None, "chan", None),
            P("chan", None, "mult"),
            P("chan", None),
            P("chan"),
            P("chan", None),
            P("chan", None),
            P("chan"),
            P(),
        ),
        out_specs=P("chan", "mult", None),
        check_vma=False,
    )
```

```python
import functools

import jax
import jax.numpy as jnp
from jax import lax
from jax.experimental import pallas as pl
from jax.experimental.pallas import tpu as pltpu
from jax.sharding import PartitionSpec as P


R = 2
SPAN = 2 * R + 1
LANES = 128
F32 = jnp.float32
BF16 = jnp.bfloat16


def ring_order(peers):
    return list(range(0, peers, 2)) + list(range(peers - 1 - peers % 2, 0, -2))


def ring_shift(value, axis, by):
    order = ring_order(lax.axis_size(axis))
    n = len(order)
    return lax.ppermute(value, axis, [(order[i], order[(i + by) % n]) for i in range(n)])


def flip(value, axis, bit):
    return lax.ppermute(value, axis, [(i, i ^ bit) for i in range(lax.axis_size(axis))])


def split(v):
    hi = v.astype(BF16)
    return hi, (v - hi.astype(F32)).astype(BF16)


def lane_group(shape, width):
    return lax.broadcasted_iota(jnp.int32, shape, len(shape) - 1) // width


def pack_kernel(col_ref, out_ref, *, kw):
    n_ch, rows, lanes = col_ref.shape
    groups = lanes // kw
    half = groups // 2
    sub = min(rows, 64)
    grp = lane_group((sub, lanes), kw)

    def share(m):
        @pl.loop(0, rows // sub)
        def _(t):
            at = pl.ds(pl.multiple_of(t * sub, sub), sub)
            re = im = None
            for j in range(n_ch):
                v = col_ref[j, at]
                if j:
                    v = pltpu.roll(v, j * kw, 1)
                re = v if re is None else jnp.where(grp == (m + j) % groups, v, re)
                im = v if im is None else jnp.where(grp == (m + half + j) % groups, v, im)
            out_ref[at, :lanes] = pltpu.roll(re, (groups - m) * kw, 1) if m else re
            out_ref[at, lanes:] = pltpu.roll(im, (half - m) * kw, 1)

    for m in range(half):
        pl.when(lax.axis_index("mult") == m)(functools.partial(share, m))


def pack(columns, kw, part):
    n_ch, nb, lanes = columns.shape
    nb, steps = nb // 2, 2
    return pl.pallas_call(
        functools.partial(pack_kernel, kw=kw),
        out_shape=jax.ShapeDtypeStruct((nb, 2 * lanes), F32),
        grid=(steps,),
        in_specs=[pl.BlockSpec((n_ch, nb // steps, lanes), lambda g: (0, part * steps + g, 0))],
        out_specs=pl.BlockSpec((nb // steps, 2 * lanes), lambda g: (g, 0)),
        name="pack",
    )(columns)


def unit_kernel(sc_ref, *refs, n_p, which, kw, steps, places, fresh, emit):
    n_x = len(places)
    p_refs, x_refs = refs[: 2 * n_p], refs[2 * n_p : 2 * (n_p + n_x)]
    a_refs = refs[2 * (n_p + n_x) : 3 * n_p + 2 * n_x]
    c_in, *c_outs, y_ref, w_ref, sem = refs[3 * n_p + 2 * n_x :]
    step = pl.program_id(0)
    n_l, _, rows, _ = p_refs[0].shape
    n_chan, _, n_ch, _ = a_refs[0].shape
    if fresh:
        fetch = None
    else:
        fetch = pltpu.make_async_copy(c_in, w_ref, sem.at[0])

    @pl.when(step == 0)
    def _():
        if fresh:
            w_ref[...] = jnp.zeros_like(w_ref)
        else:
            fetch.start()

    parts = []
    for part in range(2):
        v = jnp.concatenate(
            [
                jnp.concatenate([p_refs[2 * a + t][l, part] for t in range(2)], axis=1)
                for a in range(n_p)
                for l in range(n_l)
            ],
            axis=0,
        )
        h, l = split(v)
        parts.append((h, l))
    (rh, rl), (ih, il) = parts
    rhs = []
    for t in range(n_x):
        x = jnp.concatenate([x_refs[2 * t][...], x_refs[2 * t + 1][...]], axis=0)
        lanes = x.shape[1] // 2
        xh, xl = split(x)
        yh = jnp.concatenate([-xh[:, lanes:], xh[:, :lanes]], axis=1)
        yl = jnp.concatenate([-xl[:, lanes:], xl[:, :lanes]], axis=1)
        rhs.append((jnp.concatenate([xh, yh], axis=0), jnp.concatenate([xl, yl], axis=0)))
    hi = jnp.concatenate([rh, ih], axis=1)
    lo = jnp.concatenate([rl, il], axis=1)
    if n_x == 1:
        both = jnp.dot(hi, jnp.concatenate(rhs[0], axis=1), preferred_element_type=F32)
        prod = both[:, : 2 * lanes] + both[:, 2 * lanes :]
        prod += jnp.dot(lo, rhs[0][0], preferred_element_type=F32)
    else:
        prod = jnp.dot(
            jnp.concatenate([hi, hi, lo], axis=1),
            jnp.concatenate([jnp.concatenate([h, l, h], axis=0) for h, l in rhs], axis=1),
            preferred_element_type=F32,
        )
    for t in range(n_x):
        piece = prod[:, 2 * lanes * t : 2 * lanes * (t + 1)]

        @pl.when(step == 0)
        def _():
            y_ref[t] = piece

        @pl.when(step > 0)
        def _():
            y_ref[t] += piece

    @pl.when(step == steps - 1)
    def _():
        n = n_p * n_l
        wide = SPAN * lanes
        spread = (
            lane_group((LANES, wide), kw) == lax.broadcasted_iota(jnp.int32, (LANES, wide), 0)
        ).astype(BF16)
        same = (
            lax.broadcasted_iota(jnp.int32, (1, kw, wide), 2) % kw
            == lax.broadcasted_iota(jnp.int32, (1, kw, wide), 1)
        )
        grp = lane_group((n_ch, LANES), n_ch)

        def kron(c):
            t = jnp.dot(c, spread, preferred_element_type=F32)
            t = jnp.broadcast_to(t.astype(BF16)[:, None, :], (n * n_ch, kw, wide))
            return jnp.where(same, t, jnp.zeros_like(t)).reshape(n * n_ch * kw, wide)

        if not fresh:
            fetch.wait()

        @pl.loop(0, n_x)
        def _(t):
            s = sc_ref[places[0] + t]
            me = sc_ref[1]
            coef = []
            for a_ref, w in zip(a_refs, which):
                v = None
                for d in range(SPAN):
                    at = s + d - R
                    own = a_ref[lax.rem(me - at + 2 * n_chan, n_chan), w]
                    own = jnp.where((at >= 0) & (at < n_chan), own, 0.0)
                    v = own if v is None else jnp.where(lax.rem(grp, LANES // n_l // n_ch) == d, own, v)
                coef += [pltpu.roll(v, LANES - l * (LANES // n_l), 1) if l else v for l in range(n_l)]
            ch, cl = split(jnp.concatenate(coef, axis=0))
            kh, kl = kron(ch), kron(cl)
            y = y_ref[t]
            z = jnp.concatenate(
                [
                    jnp.concatenate(
                        [y[i * rows : (i + 1) * rows, part * lanes : (part + 1) * lanes] for i in range(n)],
                        axis=1,
                    )
                    for part in range(2)
                ],
                axis=0,
            )
            zh, zl = split(z)
            out = jnp.dot(
                jnp.concatenate([zh, zh, zl], axis=1),
                jnp.concatenate([kh, kl, kh], axis=0),
                preferred_element_type=F32,
            )
            for d in range(SPAN):
                w_ref[s + d] += out[:, d * lanes : (d + 1) * lanes]

        backs = []
        for t, c_out in enumerate(c_outs):
            block = w_ref
            if emit:
                per = n_chan // emit
                block = w_ref.at[R + lax.rem(sc_ref[0] * per + lax.rem(sc_ref[1], per) + t, n_chan)]
            backs.append(pltpu.make_async_copy(block, c_out, sem.at[1 + t]))
            backs[-1].start()
        for back in backs:
            back.wait()


def unit(total, shape, panel_sets, coefs, chunks, meta, kw, emit=0, kept=False):
    n_l, _, rows, nb = panel_sets[0].shape
    half = nb // 2
    steps = max(1, half // (2 * LANES))
    blk = half // steps
    wide = chunks[0][0].shape[1]
    n = len(panel_sets)
    in_specs, args = [], []
    for p in panel_sets:
        in_specs += [
            pl.BlockSpec((n_l, 2, rows, blk), lambda g, sc: (0, 0, 0, g)),
            pl.BlockSpec((n_l, 2, rows, blk), lambda g, sc: (0, 0, 0, steps + g)),
        ]
        args += [p, p]
    for top, bottom, _ in chunks:
        off = steps if bottom.shape[0] == nb else 0
        in_specs += [
            pl.BlockSpec((blk, wide), lambda g, sc: (g, 0)),
            pl.BlockSpec((blk, wide), lambda g, sc, off=off: (off + g, 0)),
        ]
        args += [top, bottom]
    fresh = total is None
    if fresh:
        total = coefs[0][0]
    in_specs += [pl.BlockSpec(c.shape, lambda g, sc: (0, 0, 0, 0)) for c, _ in coefs]
    in_specs += [pl.BlockSpec(memory_space=pl.ANY)]
    args += [*[c for c, _ in coefs], total]
    flops = 2 * 3 * n * n_l * rows * wide * (2 * nb + SPAN * LANES) * len(chunks)
    n_chan = shape[0] - 2 * R
    outs = [jax.ShapeDtypeStruct(shape[1:], F32)] * n_chan if emit else [jax.ShapeDtypeStruct(shape, F32)]
    result = pl.pallas_call(
        functools.partial(
            unit_kernel, n_p=n, which=tuple(w for _, w in coefs), kw=kw, steps=steps, places=tuple(c[2] for c in chunks), fresh=fresh, emit=emit
        ),
        out_shape=outs,
        grid_spec=pltpu.PrefetchScalarGridSpec(
            num_scalar_prefetch=1,
            grid=(steps,),
            in_specs=in_specs,
            out_specs=[pl.BlockSpec(memory_space=pl.ANY) for _ in outs],
            scratch_shapes=[
                pltpu.VMEM((len(chunks), n * n_l * rows, wide), F32),
                pltpu.VMEM(shape, F32),
                pltpu.SemaphoreType.DMA((1 + len(outs),)),
            ],
        ),
        input_output_aliases={} if fresh or emit else {len(args): 0},
        cost_estimate=pl.CostEstimate(
            flops=flops, transcendentals=0, bytes_accessed=4 * n * n_l * 2 * rows * nb
        ),
        compiler_params=pltpu.CompilerParams(vmem_limit_bytes=30 << 20),
        name="unit",
    )(
        meta,
        *args[: 2 * n],
        *[pltpu.with_memory_space_constraint(a, pltpu.HBM) if kept else a for a in args[2 * n : -n - 1]],
        *args[-n - 1 :],
    )
    return result if emit else result[0]


def shift_kernel(sc_ref, energy_ref, contour_ref, col_ref, out_ref):
    n_ch, rows, lanes = col_ref.shape
    upper = lax.broadcasted_iota(jnp.int32, (rows, lanes), 1) >= lanes // 2
    shift = jnp.where(upper, contour_ref[1], -contour_ref[1])
    for i in range(n_ch):
        x = col_ref[i]
        out_ref[i] = (contour_ref[0] - energy_ref[i]) * x + shift * pltpu.roll(x, lanes // 2, 1)


def shifted_columns(columns, energies, contour, meta, n_mult):
    n_ch, nb, lanes = columns.shape
    rows = nb // n_mult
    steps = max(1, rows // 64)
    sub = rows // steps
    smem = pl.BlockSpec(memory_space=pltpu.SMEM)
    return pl.pallas_call(
        shift_kernel,
        out_shape=jax.ShapeDtypeStruct((n_ch, rows, lanes), F32),
        grid_spec=pltpu.PrefetchScalarGridSpec(
            num_scalar_prefetch=1,
            grid=(steps,),
            in_specs=[smem, smem, pl.BlockSpec((n_ch, sub, lanes), lambda g, sc: (0, sc[0] * steps + g, 0))],
            out_specs=pl.BlockSpec((n_ch, sub, lanes), lambda g, sc: (0, g, 0)),
        ),
        name="shifted",
    )(meta, energies, contour, columns)


def finish_kernel(sc_ref, base_ref, *refs, kw, n_mult):
    pieces, out_ref, held = refs[:-2], refs[-2], refs[-1]
    n_ch, per, sub, lanes = base_ref.shape
    n = len(pieces)
    me = sc_ref[1]
    for s in range(n):
        held[lax.rem(me - s + n, n)] = pieces[s][...]
    groups = 2 * n_mult
    v = jnp.concatenate(
        [
            jnp.concatenate([held[u * per + h, part] for part in range(2) for u in range(n_mult)], axis=1)
            for h in range(per)
        ],
        axis=0,
    )
    vh, vl = split(v)
    both = jnp.concatenate([vh, vl], axis=0)

    row = lax.broadcasted_iota(jnp.int32, (groups * lanes, lanes), 0)
    col = lax.broadcasted_iota(jnp.int32, (groups * lanes, lanes), 1)
    start = (col // kw) * lanes + col % kw
    picks = jnp.concatenate([(row == start + i * kw).astype(BF16) for i in range(n_ch)], axis=1)
    out = jnp.dot(both, picks, preferred_element_type=F32)
    out = out[: per * sub] + out[per * sub :]
    for h in range(per):
        for i in range(n_ch):
            out_ref[i, h] = base_ref[i, h] - out[h * sub : (h + 1) * sub, i * lanes : (i + 1) * lanes]


def finish(pieces, base, meta, kw, n_mult):
    n_ch, out_rows, lanes = base.shape
    rows = pieces[0].shape[0] // 2
    per = out_rows // rows
    sub = min(rows, 64)
    out = pl.pallas_call(
        functools.partial(finish_kernel, kw=kw, n_mult=n_mult),
        out_shape=jax.ShapeDtypeStruct((n_ch, per, rows, lanes), F32),
        grid_spec=pltpu.PrefetchScalarGridSpec(
            num_scalar_prefetch=1,
            grid=(rows // sub,),
            in_specs=[pl.BlockSpec((n_ch, per, sub, lanes), lambda g, sc: (0, 0, g, 0))]
            + [pl.BlockSpec((2, sub, lanes), lambda g, sc: (0, g, 0)) for _ in pieces],
            out_specs=pl.BlockSpec((n_ch, per, sub, lanes), lambda g, sc: (0, 0, g, 0)),
            scratch_shapes=[pltpu.VMEM((len(pieces), 2, sub, lanes), F32)],
        ),
        name="finish",
    )(
        meta,
        base.reshape(n_ch, per, rows, lanes),
        *[p.reshape(2, rows, lanes) for p in pieces],
    )
    return out.reshape(n_ch, out_rows, lanes)


def after(value, *others):
    def copy_kernel(value_ref, *refs):
        refs[-1][...] = value_ref[...]

    return pl.pallas_call(
        copy_kernel,
        out_shape=jax.ShapeDtypeStruct(value.shape, value.dtype),
        in_specs=[pl.BlockSpec(memory_space=pltpu.VMEM)] + [pl.BlockSpec(memory_space=pl.ANY) for _ in others],
        out_specs=pl.BlockSpec(memory_space=pltpu.VMEM),
        name="after",
    )(value, *others)


def mixing_blocks(coefficients, channel_cols, used_slots, lambda_low, lambda_high, chan_index, mult_index):
    n_ch, slots, lam = coefficients.shape
    local = channel_cols - (chan_index - R) * n_ch
    slot_ids = jnp.arange(slots, dtype=jnp.int32)
    live = slot_ids[None, :] < used_slots[:, None]
    lambda_ids = mult_index * lam + jnp.arange(lam, dtype=jnp.int32)
    inside = (lambda_ids >= lambda_low[:, :, None]) & (lambda_ids < lambda_high[:, :, None])
    weights = jnp.where(live[:, :, None] & inside, coefficients, jnp.zeros_like(coefficients))
    lane = jnp.arange(LANES, dtype=jnp.int32)
    stride = LANES // lam
    order, dist = lane // stride, (lane % stride) // n_ch
    want = (SPAN - 1 - dist)[None, :] * n_ch + jnp.arange(n_ch, dtype=jnp.int32)[:, None]
    want = jnp.where(dist[None, :] < SPAN, want, -1)
    by_lane = jnp.tile(local.T, (1, LANES // n_ch))
    w_lane = jnp.zeros((slots, LANES), F32)
    for l in range(lam):
        w_lane = jnp.where(order[None, :] == l, jnp.tile(weights[:, :, l].T, (1, LANES // n_ch)), w_lane)
    mine = jnp.sum(
        jnp.where(by_lane[:, None, :] == want[None], w_lane[:, None, :], 0.0), axis=0
    )
    return mine


def steps_of(n_chan):
    full = (n_chan - 1) // 2
    return full, min(2, full)


def body(
    columns,
    panels,
    coefficients,
    channel_cols,
    used_slots,
    lambda_low,
    lambda_high,
    energies,
    contour,
):
    _, _, lanes = columns.shape
    n_chan, n_mult = lax.axis_size("chan"), lax.axis_size("mult")
    chan_index, mult_index = lax.axis_index("chan"), lax.axis_index("mult")
    kw = lanes // 2 // n_mult
    rows = panels.shape[2]

    seq = ring_order(n_chan)
    hops = [0]
    for step in range(1, n_chan // 2 + 1):
        hops += [-step, step]
    table = jnp.asarray(
        [[i] + [seq[(seq.index(i) + by) % n_chan] for by in hops] for i in range(n_chan)], jnp.int32
    )
    meta = jnp.concatenate([mult_index[None], table[chan_index]])

    def spot(by):
        return 2 + hops.index(by)

    mine = []
    for part in range(2):
        mine.append(pack(columns, kw, part))
    mine[1], coefficients = lax.optimization_barrier((mine[1], coefficients))
    sent = mixing_blocks(
        coefficients, channel_cols, used_slots, lambda_low, lambda_high, chan_index, mult_index
    )
    near_sent = [sent]
    bit = n_mult // 4
    while bit:
        near_sent += [flip(p, "mult", bit) for p in near_sent]
        bit //= 2
    sent = jnp.stack(near_sent)
    ahead, behind = list(mine), list(mine)

    def advance():
        for part in range(2):
            ahead[part] = ring_shift(ahead[part], "chan", 1)
            behind[part] = ring_shift(behind[part], "chan", -1)

    advance()
    gathered = [after(sent, ahead[0], behind[0])]
    for by in range(1, n_chan):
        gathered.append(
            lax.ppermute(sent, "chan", [(i, (i + by) % n_chan) for i in range(n_chan)])
        )
    gathered = jnp.stack(gathered)
    near_coefs = [(gathered, w) for w in range(len(near_sent))]

    near_sets = [panels]
    bit = n_mult // 4
    while bit:
        near_sets += [flip(p, "mult", bit) for p in near_sets]
        bit //= 2
    far = [flip(panels, "mult", n_mult // 2)]
    far_gathered = flip(gathered, "mult", n_mult // 2)
    far_coefs = [(far_gathered, w) for w in range(len(near_sent))]

    shape = (n_chan + 2 * R, 2 * rows, LANES)

    def add(total, sets, coefs, chunks, emit=0, kept=False):
        return unit(total, shape, sets, coefs, chunks, meta, kw, emit, kept)

    full_steps, switch = steps_of(n_chan)
    total = None
    held, late = [(*mine, spot(0))], []
    for step in range(1, full_steps + 1):
        if step > 1:
            advance()
        held += [(*ahead, spot(-step)), (*behind, spot(step))]
        if step <= switch:
            total = add(total, near_sets, near_coefs, held)
            late += held
        else:
            total = add(total, near_sets + far, near_coefs + far_coefs, held)
        held = []
        if step == 1:
            far[0], total = lax.optimization_barrier((far[0], total))
            bit = n_mult // 4
            while bit:
                far += [flip(p, "mult", bit) for p in far]
                bit //= 2
        if step == switch:
            total = add(total, far, far_coefs, late)
    top = ring_shift(ahead[0], "chan", 1)
    bottom = ring_shift(behind[1], "chan", -1)
    sends = add(
        total, near_sets + far, near_coefs + far_coefs, [(top, bottom, spot(n_chan // 2))], n_mult
    )

    per = n_chan // n_mult
    pieces = []
    for s in range(n_chan):
        pairs = []
        for m in range(n_mult):
            for c in range(n_chan):
                q = m * per + c % per
                pairs.append((m * n_chan + c, (c // per) * n_chan + (q + s) % n_chan))
        pieces.append(lax.ppermute(sends[s], ("mult", "chan"), pairs))
    base = shifted_columns(columns, energies, contour, meta, n_mult)
    return finish(pieces, base, meta, kw, n_mult)


def solution(mesh):
    return jax.shard_map(
        body,
        mesh=mesh,
        in_specs=(
            P("chan", None, None),
            P("mult", None, "chan", None),
            P("chan", None, "mult"),
            P("chan", None),
            P("chan"),
            P("chan", None),
            P("chan", None),
            P("chan"),
            P(),
        ),
        out_specs=P("chan", "mult", None),
        check_vma=False,
    )
```
